512 devices in a mesh: slab: 16 (over y, x), row: 32 (over z, core).
Axes of the slice: x: 4, y: 4, z: 16, core: 2. Of those that a mesh axis runs over, the one named last changes fastest.
Arguments:
- atom_feats: bfloat16 [128, 524288], P(None, ('slab', 'row')), may hold values from -6 to 6
- cotangent: bfloat16 [128, 524288], P(None, ('slab', 'row')), may hold values from -6 to 6
- filter_modes: bfloat16 [128, 256, 2, 256], P('row', 'slab'), may hold values from -5 to 5
- block_tiles: int32 [16384, 1], P(('slab', 'row')), may hold values from 0 to 31, as said below
- cell_offsets: int32 [524288], P(('slab', 'row')), may hold values from 0 to 511
- live_counts: int32 [512], P(('slab', 'row')), may hold values from 256 to 1024, as said below
Outputs:
- long_range: bfloat16 [128, 524288], P(None, ('slab', 'row'))
- grad_feats: bfloat16 [128, 524288], P(None, ('slab', 'row'))
- grad_filter: float32 [128, 256, 2, 256], P('row', 'slab')
The draws below stay inside these ranges and needn't reach their ends.
Inputs may be any that keep to these rules, and one draw needn't show every extreme that they name: `block_tiles`: in each brick's 32 blocks (the rows of one device) no x-row index appears more than 2 times; in every slab one x-row index appears exactly 2 times in every brick of that slab. `live_counts`: some brick has all 1024 slots live.
All inputs are finite; a program needn't handle non-finite values.
Results may differ from the reference program's by a relative error of at most 0.014.
Values may be sent and summed in bfloat16 or wider, within the bound.
No kernel may reach another device: no remote copies, remote signals or barrier semaphores. Data moves between devices by JAX's collectives and lax.ppermute only.
A program may use at most 64 MiB of HBM per device.

```python
import jax
import jax.numpy as jnp
from jax import lax

C = 128
NX = 256
NZ = 256
NY = 4
BLK = 32
NB = 32
A_DEV = 1024
ATOMS = 524288
CAP = 2
ZL = 16
XL = 8
TILE = 512
N_SLAB = 16
N_ROW = 32
DEVICES = 512


def draw_block_tiles(key, part):
    hot_key, device_key = jax.random.split(key)
    hot_rows = jax.random.randint(hot_key, (N_SLAB,), 0, N_ROW)
    hot_each = jnp.repeat(hot_rows, N_ROW)
    slot_targets = jnp.arange(N_ROW * CAP, dtype=jnp.int32) // CAP

    def one_device(device_seed, hot_row):
        order_key, shuffle_key = jax.random.split(device_seed)
        priority = jax.random.permutation(order_key, N_ROW * CAP).astype(jnp.int32)
        priority = jnp.where(slot_targets == hot_row, priority + N_ROW * CAP, priority)
        ordering = jnp.argsort(priority)
        remaining = slot_targets[ordering][:NB - CAP]
        chosen = jnp.concatenate([jnp.full((CAP,), hot_row, jnp.int32), remaining])
        return chosen[jax.random.permutation(shuffle_key, NB)]
    per_device = jax.vmap(one_device)(jax.random.split(device_key, DEVICES), hot_each)
    return per_device.reshape(NB * DEVICES, 1).astype(jnp.int32)


def draw_live_counts(key, part):
    draw_key, pick_key = jax.random.split(key)
    counts = jax.random.randint(draw_key, (DEVICES,), A_DEV // 4, A_DEV + 1)
    chosen = jax.random.randint(pick_key, (), 0, DEVICES)
    return jnp.where(jnp.arange(DEVICES) == chosen, A_DEV, counts).astype(jnp.int32)


def with_ends(drawn, stream_key, low, top_value):
    longest = drawn.shape.index(max(drawn.shape))
    spots = []
    for shift in (0, 1):
        where = [jax.random.randint(jax.random.fold_in(stream_key, axis), (), 0, length) for axis, length in enumerate(drawn.shape)]
        where[longest] = (where[longest] + shift) % drawn.shape[longest]
        spots.append(tuple(where))
    return drawn.at[spots[0]].set(low).at[spots[1]].set(top_value)


def level_of(rng, shape, pieces, least, top_value):
    gain = 1.0
    for axis_at, blocks in pieces:
        draws = jax.random.uniform(jax.random.fold_in(jax.random.fold_in(rng, 6), axis_at), (blocks,), jnp.float32, least / len(pieces), top_value / len(pieces))
        gain = gain * jnp.repeat(jnp.exp(draws), shape[axis_at] // blocks).reshape((-1,) + (1,) * (len(shape) - 1 - axis_at))
    return gain


def noise(key, dims, spread, reach, pieces=(), held_as=jnp.bfloat16):
    loudness = level_of(key, dims, pieces, -0.22, 0.18) if pieces else 1.0
    values = jax.random.normal(key, dims, jnp.float32) * spread * loudness
    return jnp.minimum(jnp.maximum(values, -reach), reach).astype(held_as)


def setup_inputs(seed: int = 0) -> dict:
    arg_keys = jax.random.split(jax.random.key(seed), 7)
    return {
        "atom_feats": noise(arg_keys[0], (C, ATOMS), 1.0, 6.0, ((1, 512),)),
        "cotangent": noise(arg_keys[1], (C, ATOMS), 1.0, 6.0, ((1, 512),)),
        "filter_modes": noise(arg_keys[2], (C, NX, 2, NZ), 1.0, 5.0, ((0, 32), (1, 16))),
        "block_tiles": draw_block_tiles(jax.random.fold_in(arg_keys[6], 71), 0),
        "cell_offsets": with_ends(jax.random.randint(arg_keys[4], (ATOMS,), 0, TILE), jax.random.fold_in(arg_keys[4], 1), 0, TILE - 1).astype(jnp.int32),
        "live_counts": draw_live_counts(jax.random.fold_in(arg_keys[6], 71), 0),
    }


def trig_table(length):
    positions = jnp.arange(length, dtype=jnp.int32)
    angles = ((positions[:, None] * positions[None, :]) % length).astype(jnp.float32) * (2.0 * jnp.pi / length)
    return jnp.cos(angles), jnp.sin(angles)


def make_tables():
    cos_x, sin_x = trig_table(NX)
    cos_z, sin_z = trig_table(NZ)
    inverse_size = 1.0 / (NX * NZ)
    table_fwd = jnp.concatenate([cos_x, -sin_x], axis=1).astype(jnp.bfloat16)
    table_inv = (jnp.concatenate([cos_x, -sin_x], axis=0) * inverse_size).astype(jnp.bfloat16)
    upper_half = jnp.concatenate([cos_z, -sin_z], axis=1)
    lower_half = jnp.concatenate([sin_z, cos_z], axis=1)
    table_z = jnp.concatenate([upper_half, lower_half], axis=0).astype(jnp.bfloat16)
    return table_fwd, table_inv, table_z


def to_columns(rows_in):
    arranged = rows_in.reshape(NZ, NY, 2, NX).transpose(1, 3, 2, 0)
    return arranged.reshape(NY * NX, 2 * NZ)


def to_planes(columns):
    arranged = columns.reshape(NY, NX, 2, NZ).transpose(3, 0, 2, 1)
    return arranged.reshape(NZ * NY, 2 * NX)


def reference(atom_feats, cotangent, filter_modes, block_tiles, cell_offsets, live_counts):
    table_fwd, table_inv, table_z = make_tables()
    atom_index = jnp.arange(ATOMS, dtype=jnp.int32)
    brick_index = atom_index // A_DEV
    live_mask = (atom_index % A_DEV) < live_counts[brick_index]
    target = block_tiles[atom_index // BLK, 0]
    offset = cell_offsets
    z_cell = (brick_index // N_ROW) * ZL + offset // (NY * XL)
    y_cell = (offset // XL) % NY
    x_cell = target * XL + offset % XL
    flat_cell = ((z_cell * NY + y_cell) * NX + x_cell).astype(jnp.int32)

    def spread_one(values):
        kept_values = jnp.where(live_mask, values.astype(jnp.float32), jnp.float32(0.0))
        summed = jnp.zeros((NZ * NY * NX,), jnp.float32).at[flat_cell].add(kept_values)
        return summed.astype(jnp.bfloat16).reshape(NZ * NY, NX)

    def channel(inputs):
        feat_column, cot_column, filter_one = inputs
        mesh_feats = spread_one(feat_column)
        mesh_cot = spread_one(cot_column)
        row_feats = jnp.dot(mesh_feats, table_fwd, preferred_element_type=jnp.float32).astype(jnp.bfloat16)
        row_cot = jnp.dot(mesh_cot, table_inv.T, preferred_element_type=jnp.float32).astype(jnp.bfloat16)
        spectrum = jnp.dot(to_columns(row_feats), table_z, preferred_element_type=jnp.float32).astype(jnp.bfloat16)
        cot_filtered = jnp.dot(to_columns(row_cot), table_z, preferred_element_type=jnp.float32).astype(jnp.bfloat16)
        spec_four = spectrum.reshape(NY, NX, 2, NZ).astype(jnp.float32)
        grad_four = cot_filtered.reshape(NY, NX, 2, NZ).astype(jnp.float32)
        real_s = spec_four[:, :, 0, :]
        imag_s = spec_four[:, :, 1, :]
        real_g = grad_four[:, :, 0, :]
        imag_g = grad_four[:, :, 1, :]
        filter_f32 = filter_one.astype(jnp.float32)
        real_f = filter_f32[None, :, 0, :]
        imag_f = filter_f32[None, :, 1, :]
        filtered = jnp.stack([real_s * real_f - imag_s * imag_f, real_s * imag_f + imag_s * real_f], axis=2)
        filtered = filtered.astype(jnp.bfloat16).reshape(NY * NX, 2 * NZ)
        grad_filter = jnp.stack([jnp.sum(real_g * real_s + imag_g * imag_s, axis=0),
                                 jnp.sum(imag_g * real_s - real_g * imag_s, axis=0)], axis=1)
        cot_spectrum = jnp.stack([real_g * real_f + imag_g * imag_f, imag_g * real_f - real_g * imag_f], axis=2)
        cot_spectrum = cot_spectrum.astype(jnp.bfloat16).reshape(NY * NX, 2 * NZ)
        planes = jnp.dot(filtered, table_z.T, preferred_element_type=jnp.float32).astype(jnp.bfloat16)
        cot_planes = jnp.dot(cot_spectrum, table_z.T, preferred_element_type=jnp.float32).astype(jnp.bfloat16)
        field_flat = jnp.dot(to_planes(planes), table_inv, preferred_element_type=jnp.float32).astype(jnp.bfloat16).reshape(-1)
        cot_field = jnp.dot(to_planes(cot_planes), table_fwd.T, preferred_element_type=jnp.float32).astype(jnp.bfloat16).reshape(-1)
        at_atoms = field_flat[flat_cell]
        cot_atoms = cot_field[flat_cell]
        long_range = jnp.where(live_mask, at_atoms, jnp.zeros_like(at_atoms))
        grad_feats = jnp.where(live_mask, cot_atoms, jnp.zeros_like(cot_atoms))
        return long_range, grad_feats, grad_filter

    long_range, grad_feats, grad_filter = lax.map(channel, (atom_feats, cotangent, filter_modes))
    return long_range, grad_feats, grad_filter
```

```python
import jax
import jax.numpy as jnp
import numpy as np
from jax import lax
from jax.experimental import pallas as pl
from jax.experimental.pallas import tpu as pltpu
from jax.sharding import PartitionSpec as P

C = 128
NX = 256
NZ = 256
NY = 4
BLK = 32
N_SLAB = 16
N_ROW = 32
CL = C // N_ROW
KX = NX // N_SLAB
ZL = NZ // N_SLAB
A_DEV = 1024
LT = A_DEV // 128
ROWS = CL * NY * ZL
INV = 1.0 / (NX * NZ)
BF = jnp.bfloat16
F32 = jnp.float32
NT = (((1,), (1,)), ((), ()))
TN = (((0,), (0,)), ((), ()))
NN = (((1,), (0,)), ((), ()))
VMEM = pl.BlockSpec(memory_space=pltpu.VMEM)
PARAMS = pltpu.CompilerParams(vmem_limit_bytes=24 << 20)


def trig_table(length):
    n = np.arange(length)
    angles = (np.outer(n, n) % length) * (2.0 * np.pi / length)
    return np.cos(angles), np.sin(angles)


def make_tables():
    cos_x, sin_x = trig_table(NX)
    cos_z, sin_z = trig_table(NZ)
    table_x = np.concatenate([cos_x, -sin_x], axis=1)
    upper = np.concatenate([cos_z, -sin_z], axis=1)
    lower = np.concatenate([sin_z, cos_z], axis=1)
    table_z = np.concatenate([upper, lower], axis=0)
    table_z = table_z.reshape(2, N_SLAB, ZL, 2 * NZ).transpose(1, 0, 2, 3).reshape(2 * NZ, 2 * NZ)
    return jnp.asarray(table_x.astype(np.float32)).astype(BF), jnp.asarray(
        table_z.astype(np.float32)
    ).astype(BF)


def swap_chunks(parts):
    parts = list(parts)
    chunk = lax.broadcasted_iota(jnp.int32, parts[0].shape, 1) // KX
    for step in (1, 2, 4):
        upper = (chunk & step) != 0
        for i in range(8):
            if i & step:
                continue
            first, second = parts[i], parts[i | step]
            parts[i] = jnp.where(upper, pltpu.roll(second, step * KX, 1), first)
            parts[i | step] = jnp.where(upper, second, pltpu.roll(first, 128 - step * KX, 1))
    return parts


def encode_cells(cells, live):
    value = 1.0 + (cells & 127).astype(F32) * (1.0 / 128.0)
    for bit in range(6):
        value = value * jnp.where((cells >> (7 + bit)) & 1 == 1, 2.0 ** (1 << bit), 1.0)
    value = value * jnp.where((cells >> 13) & 1 == 1, 1.0, 2.0**-64)
    return jnp.where(live, value, 0.0).astype(BF)


def decode_cells(code):
    value = code.astype(F32)
    live = value > 0.0
    top = value >= 1.0
    value = jnp.where(top, value, value * 2.0**64)
    high = jnp.where(top, 64, 0)
    for bit in range(5, -1, -1):
        over = value >= 2.0 ** (1 << bit)
        value = jnp.where(over, value * 2.0 ** -(1 << bit), value)
        high = high + jnp.where(over, 1 << bit, 0)
    low = ((value - 1.0) * 128.0).astype(jnp.int32)
    return jnp.where(live, high * 128 + low, -1)


def one_hot_x(x_cell, j):
    line = lax.broadcasted_iota(jnp.int32, (NX, 128), 0)
    return jnp.where(jnp.broadcast_to(x_cell[j : j + 1], (NX, 128)) == line, 1.0, 0.0).astype(BF)


def zy_mask(zy_cell, j):
    line = lax.broadcasted_iota(jnp.int32, (NY * ZL, 128), 0)
    return jnp.broadcast_to(zy_cell[j : j + 1], (NY * ZL, 128)) == line


def spread_kernel(scale, value_ref, code_ref, table_ref, out_ref, acc_ref):
    acc_ref[...] = jnp.zeros_like(acc_ref)

    def one_brick(src, carry):
        cells = decode_cells(code_ref[src, CL * LT : (CL + 1) * LT, :])
        zy_cell, x_cell = cells >> 8, cells & (NX - 1)
        values = value_ref[src, 0 : CL * LT, :].astype(F32)
        left, right = [], []
        for j in range(LT):
            mask = zy_mask(zy_cell, j)
            right.append(one_hot_x(x_cell, j))
            left.append(
                jnp.concatenate(
                    [
                        jnp.where(
                            mask,
                            jnp.broadcast_to(values[c * LT + j : c * LT + j + 1], mask.shape),
                            0.0,
                        ).astype(BF)
                        for c in range(CL)
                    ],
                    axis=0,
                )
            )
        acc_ref[...] += lax.dot_general(
            jnp.concatenate(left, axis=1),
            jnp.concatenate(right, axis=1),
            NT,
            preferred_element_type=F32,
        )
        return carry

    lax.fori_loop(0, N_ROW, one_brick, 0)
    rows = jnp.dot(acc_ref[...].astype(BF), table_ref[...], preferred_element_type=F32)
    if scale != 1.0:
        rows = rows * scale
    for part in range(2):
        for group in range(CL * NY // 8):
            for half in range(2):
                lanes = part * NX + half * 128
                chunks = swap_chunks(
                    [
                        rows[(group * 8 + i) * ZL : (group * 8 + i + 1) * ZL, lanes : lanes + 128]
                        for i in range(8)
                    ]
                )
                for j in range(8):
                    out_ref[
                        half * 8 + j, part * ZL : (part + 1) * ZL, group * 128 : (group + 1) * 128
                    ] = chunks[j].astype(BF)


def spread(values, codes, table_x, scale):
    return pl.pallas_call(
        lambda *refs: spread_kernel(scale, *refs),
        out_shape=jax.ShapeDtypeStruct((N_SLAB, 2 * ZL, CL * NY * KX), BF),
        in_specs=[VMEM] * 3,
        out_specs=VMEM,
        scratch_shapes=[pltpu.VMEM((ROWS, NX), F32)],
        compiler_params=PARAMS,
        name="spread",
    )(values, codes, table_x)


def spectral_kernel(feat_ref, cot_ref, table_ref, filter_ref, out_f_ref, out_c_ref, grad_ref):
    table = table_ref[...]
    lines = CL * NY * KX

    def to_modes(ref):
        flat = ref[...].reshape(2 * NZ, lines)
        return lax.dot_general(flat, table, TN, preferred_element_type=F32).astype(BF).astype(F32)

    spec, cot = to_modes(feat_ref), to_modes(cot_ref)
    filtered, cot_spec = [], []
    for c in range(CL):
        filt = filter_ref[c * KX : (c + 1) * KX, :].astype(F32)
        fr, fi = filt[:, :NZ], filt[:, NZ:]
        grad_r = jnp.zeros((KX, NZ), F32)
        grad_i = jnp.zeros((KX, NZ), F32)
        for y in range(NY):
            rows = slice((c * NY + y) * KX, (c * NY + y + 1) * KX)
            sr, si = spec[rows, :NZ], spec[rows, NZ:]
            gr, gi = cot[rows, :NZ], cot[rows, NZ:]
            filtered.append(jnp.concatenate([sr * fr - si * fi, sr * fi + si * fr], axis=1).astype(BF))
            cot_spec.append(jnp.concatenate([gr * fr + gi * fi, gi * fr - gr * fi], axis=1).astype(BF))
            grad_r = grad_r + (gr * sr + gi * si)
            grad_i = grad_i + (gi * sr - gr * si)
        grad_ref[c * KX : (c + 1) * KX, :NZ] = grad_r
        grad_ref[c * KX : (c + 1) * KX, NZ:] = grad_i
    for parts, ref in ((filtered, out_f_ref), (cot_spec, out_c_ref)):
        planes = lax.dot_general(
            table, jnp.concatenate(parts, axis=0), NT, preferred_element_type=F32
        )
        ref[...] = planes.astype(BF).reshape(ref.shape)


def spectral(feat_cols, cot_cols, table_z, filters):
    shape = jax.ShapeDtypeStruct((N_SLAB, 2 * ZL, CL * NY * KX), BF)
    return pl.pallas_call(
        spectral_kernel,
        out_shape=(shape, shape, jax.ShapeDtypeStruct((CL * KX, 2 * NZ), F32)),
        in_specs=[VMEM] * 4,
        out_specs=(VMEM,) * 3,
        compiler_params=PARAMS,
        name="spectral",
    )(feat_cols, cot_cols, table_z, filters)


def gather_kernel(scale, plane_ref, code_ref, table_ref, out_ref, rows_ref):
    for part in range(2):
        for group in range(CL * NY // 8):
            for half in range(2):
                chunks = swap_chunks(
                    [
                        plane_ref[
                            half * 8 + j,
                            part * ZL : (part + 1) * ZL,
                            group * 128 : (group + 1) * 128,
                        ].astype(F32)
                        for j in range(8)
                    ]
                )
                lanes = part * NX + half * 128
                for i in range(8):
                    rows_ref[
                        (group * 8 + i) * ZL : (group * 8 + i + 1) * ZL, lanes : lanes + 128
                    ] = chunks[i].astype(BF)
    field = lax.dot_general(rows_ref[...], table_ref[...], NT, preferred_element_type=F32)
    if scale != 1.0:
        field = field * scale
    field = field.astype(BF)
    sub = lax.broadcasted_iota(jnp.int32, (LT, 128), 0)

    def one_brick(src, carry):
        cells = decode_cells(code_ref[src, CL * LT : (CL + 1) * LT, :])
        zy_cell, x_cell = cells >> 8, cells & (NX - 1)
        picks = jnp.concatenate([one_hot_x(x_cell, j) for j in range(LT)], axis=1)
        lines = jnp.dot(field, picks, preferred_element_type=F32)
        found = [jnp.zeros((LT, 128), F32) for _ in range(CL)]
        for j in range(LT):
            mask = zy_mask(zy_cell, j)
            for c in range(CL):
                line = lines[c * NY * ZL : (c + 1) * NY * ZL, j * 128 : (j + 1) * 128]
                total = jnp.sum(jnp.where(mask, line, 0.0), axis=0, keepdims=True)
                found[c] = jnp.where(sub == j, jnp.broadcast_to(total, (LT, 128)), found[c])
        out_ref[src] = jnp.concatenate(found, axis=0).astype(BF)
        return carry

    lax.fori_loop(0, N_ROW, one_brick, 0)


def gather(planes, codes, table_x, scale):
    return pl.pallas_call(
        lambda *refs: gather_kernel(scale, *refs),
        out_shape=jax.ShapeDtypeStruct((N_ROW, CL * LT, 128), BF),
        in_specs=[VMEM] * 3,
        out_specs=VMEM,
        scratch_shapes=[pltpu.VMEM((ROWS, 2 * NX), BF)],
        compiler_params=PARAMS,
        name="gather",
    )(planes, codes, table_x)


def atom_codes(block_tiles, cell_offsets, live_counts):
    slot = jnp.arange(A_DEV, dtype=jnp.int32)
    tile = jnp.broadcast_to(block_tiles, (A_DEV // BLK, BLK)).reshape(A_DEV)
    offset = cell_offsets
    zy_cell = ((offset >> 3) & (NY - 1)) * ZL + (offset >> 5)
    cells = zy_cell * NX + tile * (NX // N_ROW) + (offset & 7)
    return encode_cells(cells, slot < live_counts[0])


def on_device(atom_feats, cotangent, filter_modes, block_tiles, cell_offsets, live_counts):
    table_x, table_z = make_tables()
    code = atom_codes(block_tiles, cell_offsets, live_counts).reshape(1, LT, 128)
    feats = jnp.concatenate(
        [
            atom_feats.reshape(N_ROW, CL * LT, 128),
            jnp.broadcast_to(code, (N_ROW, LT, 128)),
        ],
        axis=1,
    )
    cots = cotangent.reshape(N_ROW, CL * LT, 128)

    def over(axis, values):
        return lax.all_to_all(values, axis, split_axis=0, concat_axis=0, tiled=True)

    got_feats = over("row", feats)
    got_cots = over("row", cots)
    feat_cols = over("slab", spread(got_feats, got_feats, table_x, 1.0))
    cot_cols = over("slab", spread(got_cots, got_feats, table_x, INV))
    filters = filter_modes.reshape(CL * KX, 2 * NZ)
    planes, cot_planes, grad = spectral(feat_cols, cot_cols, table_z, filters)
    field_vals = gather(over("slab", planes), got_feats, table_x, INV)
    cot_vals = gather(over("slab", cot_planes), got_feats, table_x, 1.0)
    long_range = over("row", field_vals).reshape(C, A_DEV)
    grad_feats = over("row", cot_vals).reshape(C, A_DEV)
    return (long_range, grad_feats, grad.reshape(CL, KX, 2, NZ))


def solution(mesh):
    in_specs = (
        P(None, ("slab", "row")),
        P(None, ("slab", "row")),
        P("row", "slab", None, None),
        P(("slab", "row"), None),
        P(("slab", "row")),
        P(("slab", "row")),
    )
    out_specs = (P(None, ("slab", "row")), P(None, ("slab", "row")), P("row", "slab", None, None))
    return jax.shard_map(
        on_device, mesh=mesh, in_specs=in_specs, out_specs=out_specs, check_vma=False
    )
```

```python
import jax
import jax.numpy as jnp
import numpy as np
from jax import lax
from jax.experimental import pallas as pl
from jax.experimental.pallas import tpu as pltpu
from jax.sharding import PartitionSpec as P

C = 128
NX = 256
NZ = 256
NY = 4
BLK = 32
N_SLAB = 16
N_ROW = 32
CL = C // N_ROW
FC = 2 * CL
KX = NX // N_SLAB
ZL = NZ // N_SLAB
A_DEV = 1024
LT = A_DEV // 128
BLOCKS = A_DEV // BLK
ZY = NY * ZL
HALF = CL * ZY
LINES = CL * NY * KX
INV = 1.0 / (NX * NZ)
PACK = 16
ROWS = N_ROW * LT
GROUP = 16
LIST = ROWS + GROUP + LT
BF = jnp.bfloat16
F32 = jnp.float32
NT = (((1,), (1,)), ((), ()))
TN = (((0,), (0,)), ((), ()))
VMEM = pl.BlockSpec(memory_space=pltpu.VMEM)
SMEM = pl.BlockSpec(memory_space=pltpu.SMEM)
PARAMS = pltpu.CompilerParams(vmem_limit_bytes=32 << 20)


def trig_table(length):
    n = np.arange(length)
    angles = (np.outer(n, n) % length) * (2.0 * np.pi / length)
    return np.cos(angles), np.sin(angles)


def make_tables():
    cos_x, sin_x = trig_table(NX)
    cos_z, sin_z = trig_table(NZ)
    table_x = np.concatenate([cos_x, -sin_x], axis=1)
    upper = np.concatenate([cos_z, -sin_z], axis=1)
    lower = np.concatenate([sin_z, cos_z], axis=1)
    table_z = np.concatenate([upper, lower], axis=0)
    table_z = table_z.reshape(2, N_SLAB, ZL, 2 * NZ).transpose(1, 0, 2, 3).reshape(2 * NZ, 2 * NZ)
    return jnp.asarray(table_x.astype(np.float32)).astype(BF), jnp.asarray(
        table_z.astype(np.float32)
    ).astype(BF)


def swap_chunks(parts):
    parts = list(parts)
    chunk = lax.broadcasted_iota(jnp.int32, parts[0].shape, 1) // KX
    for step in (1, 2, 4):
        upper = (chunk & step) != 0
        for i in range(8):
            if i & step:
                continue
            first, second = parts[i], parts[i | step]
            parts[i] = jnp.where(upper, pltpu.roll(second, step * KX, 1), first)
            parts[i | step] = jnp.where(upper, second, pltpu.roll(first, 128 - step * KX, 1))
    return parts


def encode_cells(cells, live):
    value = 1.0 + (cells & 127).astype(F32) * (1.0 / 128.0)
    for bit in range(6):
        value = value * jnp.where((cells >> (7 + bit)) & 1 == 1, F32(2.0 ** (1 << bit)), F32(1.0))
    value = value * jnp.where((cells >> 13) & 1 == 1, F32(1.0), F32(2.0**-64))
    return jnp.where(live, value, 0.0).astype(BF)


def decode_cells(code):
    value = code.astype(F32)
    live = value > 0.0
    top = value >= 1.0
    value = jnp.where(top, value, value * 2.0**64)
    high = jnp.where(top, 64, 0)
    for bit in range(5, -1, -1):
        over = value >= 2.0 ** (1 << bit)
        value = jnp.where(over, value * 2.0 ** -(1 << bit), value)
        high = high + jnp.where(over, 1 << bit, 0)
    low = ((value - 1.0) * 128.0).astype(jnp.int32)
    return jnp.where(live, high * 128 + low, -1)


def pack_kernel(tile_ref, live_ref, feat_ref, cot_ref, offset_ref, out_ref):
    shape = (LT, 128)
    slot = lax.broadcasted_iota(jnp.int32, shape, 0) * 128 + lax.broadcasted_iota(
        jnp.int32, shape, 1
    )
    block = slot // BLK
    tile = jnp.zeros(shape, jnp.int32)
    for n in range(BLOCKS):
        tile = jnp.where(block == n, tile_ref[n], tile)
    offset = offset_ref[...]
    zy_cell = ((offset >> 3) & (NY - 1)) * ZL + (offset >> 5)
    cells = zy_cell * NX + tile * (NX // N_ROW) + (offset & 7)
    code = encode_cells(cells, slot < live_ref[0])
    low = lax.broadcasted_iota(jnp.int32, (FC, 128), 0) < CL
    for j in range(LT):
        lanes = slice(j * 128, (j + 1) * 128)
        for pair in range(N_ROW // 2):
            rows = slice(pair * FC, (pair + 1) * FC)
            feat = feat_ref[rows, lanes].astype(F32)
            cot = cot_ref[rows, lanes].astype(F32)
            out_ref[2 * pair, j] = jnp.where(low, feat, pltpu.roll(cot, CL, 0)).astype(BF)
            out_ref[2 * pair + 1, j] = jnp.where(low, pltpu.roll(feat, CL, 0), cot).astype(BF)
    for owner in range(N_ROW):
        out_ref[owner, LT] = code


def pack(atom_feats, cotangent, block_tiles, cell_offsets, live_counts):
    return pl.pallas_call(
        pack_kernel,
        out_shape=jax.ShapeDtypeStruct((N_ROW, LT + 1, FC, 128), BF),
        in_specs=[SMEM, SMEM, VMEM, VMEM, VMEM],
        out_specs=VMEM,
        compiler_params=PARAMS,
        name="pack",
    )(
        block_tiles.reshape(BLOCKS),
        live_counts,
        atom_feats,
        cotangent,
        cell_offsets.reshape(LT, 128),
    )


def unpack_kernel(in_ref, feat_ref, cot_ref):
    low = lax.broadcasted_iota(jnp.int32, (FC, 128), 0) < CL
    for j in range(LT):
        lanes = slice(j * 128, (j + 1) * 128)
        for pair in range(N_ROW // 2):
            rows = slice(pair * FC, (pair + 1) * FC)
            first = in_ref[2 * pair, j].astype(F32)
            second = in_ref[2 * pair + 1, j].astype(F32)
            feat_ref[rows, lanes] = jnp.where(low, first, pltpu.roll(second, CL, 0)).astype(BF)
            cot_ref[rows, lanes] = jnp.where(low, pltpu.roll(first, CL, 0), second).astype(BF)


def unpack(values):
    shape = jax.ShapeDtypeStruct((C, A_DEV), BF)
    return pl.pallas_call(
        unpack_kernel,
        out_shape=(shape, shape),
        in_specs=[VMEM],
        out_specs=(VMEM, VMEM),
        compiler_params=PARAMS,
        name="unpack",
    )(values)


def on_rows(row, dtype):
    return jnp.broadcast_to(row, (PACK, 128)).astype(dtype)


def line_numbers(count, dtype):
    return [
        (lax.broadcasted_iota(jnp.int32, (PACK, 128), 0) + first).astype(F32).astype(dtype)
        for first in range(0, count, PACK)
    ]


def one_hot_x(x_row, lines):
    cell = on_rows(x_row, BF)
    one, zero = jnp.ones((PACK, 128), BF), jnp.zeros((PACK, 128), BF)
    return jnp.concatenate([jnp.where(cell == line, one, zero) for line in lines], axis=0)


def sum_rows(blocks):
    sub = lax.broadcasted_iota(jnp.int32, (8, 128), 0)
    low = (sub & 4) == 0
    blocks = [
        jnp.where(low, first, second) + pltpu.roll(jnp.where(low, second, first), 4, 0)
        for first, second in zip(blocks[:4], blocks[4:])
    ]
    for step in (2, 1):
        low = (sub & step) == 0
        blocks = [
            jnp.where(low, first + pltpu.roll(first, 8 - step, 0), second + pltpu.roll(second, step, 0))
            for first, second in zip(blocks[:step], blocks[step:])
        ]
    return blocks[0]


def spread_kernel(got_ref, table_ref, out_ref, list_ref, zy_ref, x_ref, acc_ref):
    first_lane = lax.broadcasted_iota(jnp.int32, (LT, 128), 1) == 0
    zy_ref[ROWS : ROWS + LT, :] = jnp.full((LT, 128), -1.0, F32)
    x_ref[ROWS : ROWS + LT, :] = jnp.zeros((LT, 128), F32)
    total = jnp.int32(0)
    for src in range(N_ROW):
        cells = decode_cells(got_ref[src, LT])
        rows = slice(src * LT, (src + 1) * LT)
        zy_ref[rows, :] = (cells >> 8).astype(F32)
        x_ref[rows, :] = (cells & (NX - 1)).astype(F32)
        live_rows = jnp.sum(jnp.where(first_lane & (cells >= 0), 1.0, 0.0)).astype(jnp.int32)
        for j in range(LT):
            list_ref[total + j] = src * LT + j
        total = total + live_rows
    for n in range(GROUP):
        list_ref[total + n] = ROWS
    steps = (total + GROUP - 1) // GROUP
    list_ref[LIST - 1] = steps

    acc_ref[...] = jnp.zeros_like(acc_ref)
    zero = jnp.zeros((PACK, 128), BF)

    def some_rows(step, carry):
        x_lines, zy_lines = line_numbers(NX, BF), line_numbers(ZY, BF)
        left, right = [], []
        for n in range(GROUP):
            row = list_ref[step * GROUP + n]
            held = jnp.minimum(row, ROWS - 1)
            values = got_ref[held // LT, held % LT].astype(F32)
            cell = on_rows(zy_ref[pl.ds(row, 1), :], BF)
            masks = [cell == line for line in zy_lines]
            right.append(one_hot_x(x_ref[pl.ds(row, 1), :], x_lines))
            parts = []
            for c in range(FC):
                value = on_rows(values[c : c + 1], BF)
                parts += [jnp.where(mask, value, zero) for mask in masks]
            left.append(jnp.concatenate(parts, axis=0))
        acc_ref[...] += lax.dot_general(
            jnp.concatenate(left, axis=1),
            jnp.concatenate(right, axis=1),
            NT,
            preferred_element_type=F32,
        )
        return carry

    lax.fori_loop(0, steps, some_rows, 0)
    for field in range(2):
        rows = jnp.dot(
            acc_ref[field * HALF : (field + 1) * HALF, :].astype(BF),
            table_ref[...],
            preferred_element_type=F32,
        )
        if field == 1:
            rows = rows * INV
        for part in range(2):
            for group in range(CL * NY // 8):
                for half in range(2):
                    lanes = part * NX + half * 128
                    chunks = swap_chunks(
                        [
                            rows[(group * 8 + i) * ZL : (group * 8 + i + 1) * ZL, lanes : lanes + 128]
                            for i in range(8)
                        ]
                    )
                    place = field * LINES + group * 128
                    for j in range(8):
                        out_ref[
                            half * 8 + j, part * ZL : (part + 1) * ZL, place : place + 128
                        ] = chunks[j].astype(BF)


def spread(got, table_x):
    cells = jax.ShapeDtypeStruct((ROWS + LT, 128), F32)
    return pl.pallas_call(
        spread_kernel,
        out_shape=(
            jax.ShapeDtypeStruct((N_SLAB, 2 * ZL, 2 * LINES), BF),
            jax.ShapeDtypeStruct((LIST,), jnp.int32),
            cells,
            cells,
        ),
        in_specs=[VMEM] * 2,
        out_specs=(VMEM, SMEM, VMEM, VMEM),
        scratch_shapes=[pltpu.VMEM((2 * HALF, NX), F32)],
        compiler_params=PARAMS,
        name="spread",
    )(got, table_x)


def spectral_kernel(cols_ref, table_ref, filter_ref, out_ref, grad_ref, mode_ref):
    table = table_ref[...]
    cols = cols_ref[...].reshape(2 * NZ, 2 * LINES)
    mode_ref[...] = lax.dot_general(cols, table, TN, preferred_element_type=F32).astype(BF)
    filtered, cot_spec = [], []
    for c in range(CL):
        filt = filter_ref[c * KX : (c + 1) * KX, :].astype(F32)
        fr, fi = filt[:, :NZ], filt[:, NZ:]
        grad_r = jnp.zeros((KX, NZ), F32)
        grad_i = jnp.zeros((KX, NZ), F32)
        for y in range(NY):
            first = (c * NY + y) * KX
            spec = mode_ref[first : first + KX, :].astype(F32)
            cot = mode_ref[LINES + first : LINES + first + KX, :].astype(F32)
            sr, si = spec[:, :NZ], spec[:, NZ:]
            gr, gi = cot[:, :NZ], cot[:, NZ:]
            filtered.append(jnp.concatenate([sr * fr - si * fi, sr * fi + si * fr], axis=1).astype(BF))
            cot_spec.append(jnp.concatenate([gr * fr + gi * fi, gi * fr - gr * fi], axis=1).astype(BF))
            grad_r = grad_r + (gr * sr + gi * si)
            grad_i = grad_i + (gi * sr - gr * si)
        grad_ref[c * KX : (c + 1) * KX, :NZ] = grad_r
        grad_ref[c * KX : (c + 1) * KX, NZ:] = grad_i
    for field, parts in enumerate((filtered, cot_spec)):
        planes = lax.dot_general(
            table, jnp.concatenate(parts, axis=0), NT, preferred_element_type=F32
        )
        out_ref[:, :, field * LINES : (field + 1) * LINES] = planes.astype(BF).reshape(
            N_SLAB, 2 * ZL, LINES
        )


def spectral(cols, table_z, filters):
    return pl.pallas_call(
        spectral_kernel,
        out_shape=(
            jax.ShapeDtypeStruct((N_SLAB, 2 * ZL, 2 * LINES), BF),
            jax.ShapeDtypeStruct((CL * KX, 2 * NZ), F32),
        ),
        in_specs=[VMEM] * 3,
        out_specs=(VMEM,) * 2,
        scratch_shapes=[pltpu.VMEM((2 * LINES, 2 * NZ), BF)],
        compiler_params=PARAMS,
        name="spectral",
    )(cols, table_z, filters)


def gather_kernel(list_ref, plane_ref, table_ref, zy_ref, x_ref, out_ref, mode_ref, field_ref):
    for field in range(2):
        for part in range(2):
            for group in range(CL * NY // 8):
                place = field * LINES + group * 128
                for half in range(2):
                    chunks = swap_chunks(
                        [
                            plane_ref[
                                half * 8 + j, part * ZL : (part + 1) * ZL, place : place + 128
                            ].astype(F32)
                            for j in range(8)
                        ]
                    )
                    lanes = part * NX + half * 128
                    for i in range(8):
                        first = field * HALF + (group * 8 + i) * ZL
                        mode_ref[first : first + ZL, lanes : lanes + 128] = chunks[i].astype(BF)
    cells = lax.dot_general(mode_ref[...], table_ref[...], NT, preferred_element_type=F32)
    field_ref[:HALF, :] = (cells[:HALF] * INV).astype(BF)
    field_ref[HALF:, :] = cells[HALF:].astype(BF)
    out_ref[...] = jnp.zeros_like(out_ref)
    zy_line = lax.broadcasted_iota(jnp.int32, (8, 128), 0).astype(F32)

    def some_rows(step, carry):
        x_lines = line_numbers(NX, BF)
        for pair in range(0, GROUP, 2):
            rows = []
            for n in (pair, pair + 1):
                row = list_ref[step * GROUP + n]
                rows.append(jnp.where(row == ROWS, 0, row))
            picks = jnp.concatenate(
                [one_hot_x(x_ref[pl.ds(row, 1), :], x_lines) for row in rows], axis=1
            )
            lines = jnp.dot(field_ref[...], picks, preferred_element_type=F32)
            for n, row in enumerate(rows):
                cell = jnp.broadcast_to(zy_ref[pl.ds(row, 1), :], (8, 128))
                masks = [cell == zy_line + first for first in range(0, ZY, 8)]
                found = []
                for c in range(FC):
                    kept = jnp.zeros((8, 128), F32)
                    for k, mask in enumerate(masks):
                        first = c * ZY + k * 8
                        kept = jnp.where(
                            mask, lines[first : first + 8, n * 128 : (n + 1) * 128], kept
                        )
                    found.append(kept)
                out_ref[row // LT, row % LT] = sum_rows(found).astype(BF)
        return carry

    lax.fori_loop(0, list_ref[LIST - 1], some_rows, 0)


def gather(rows, planes, table_x, zy_cells, x_cells):
    return pl.pallas_call(
        gather_kernel,
        out_shape=jax.ShapeDtypeStruct((N_ROW, LT, FC, 128), BF),
        in_specs=[SMEM] + [VMEM] * 4,
        out_specs=VMEM,
        scratch_shapes=[pltpu.VMEM((2 * HALF, 2 * NX), BF), pltpu.VMEM((2 * HALF, NX), BF)],
        compiler_params=PARAMS,
        name="gather",
    )(rows, planes, table_x, zy_cells, x_cells)


def on_device(atom_feats, cotangent, filter_modes, block_tiles, cell_offsets, live_counts):
    table_x, table_z = make_tables()

    def over(axis, values):
        return lax.all_to_all(values, axis, split_axis=0, concat_axis=0, tiled=True)

    got = over("row", pack(atom_feats, cotangent, block_tiles, cell_offsets, live_counts))
    cols, rows, zy_cells, x_cells = spread(got, table_x)
    planes, grad = spectral(over("slab", cols), table_z, filter_modes.reshape(CL * KX, 2 * NZ))
    found = gather(rows, over("slab", planes), table_x, zy_cells, x_cells)
    long_range, grad_feats = unpack(over("row", found))
    return (long_range, grad_feats, grad.reshape(CL, KX, 2, NZ))


def solution(mesh):
    in_specs = (
        P(None, ("slab", "row")),
        P(None, ("slab", "row")),
        P("row", "slab", None, None),
        P(("slab", "row"), None),
        P(("slab", "row")),
        P(("slab", "row")),
    )
    out_specs = (P(None, ("slab", "row")), P(None, ("slab", "row")), P("row", "slab", None, None))
    return jax.shard_map(
        on_device, mesh=mesh, in_specs=in_specs, out_specs=out_specs, check_vma=False
    )
```

```python
import jax
import jax.numpy as jnp
import numpy as np
from jax import lax
from jax.experimental import pallas as pl
from jax.experimental.pallas import tpu as pltpu
from jax.sharding import PartitionSpec as P

C = 128
NX = 256
NZ = 256
NY = 4
BLK = 32
N_SLAB = 16
N_ROW = 32
CL = C // N_ROW
FC = 2 * CL
KX = NX // N_SLAB
ZL = NZ // N_SLAB
A_DEV = 1024
LT = A_DEV // 128
BLOCKS = A_DEV // BLK
ZY = NY * ZL
HALF = CL * ZY
LINES = CL * NY * KX
INV = 1.0 / (NX * NZ)
PACK = 16
ROWS = N_ROW * LT
GROUP = 16
PIECES = 4
LIST = ROWS + GROUP + LT
BF = jnp.bfloat16
F32 = jnp.float32
NT = (((1,), (1,)), ((), ()))
TN = (((0,), (0,)), ((), ()))
VMEM = pl.BlockSpec(memory_space=pltpu.VMEM)
SMEM = pl.BlockSpec(memory_space=pltpu.SMEM)
HBM = pl.BlockSpec(memory_space=pltpu.HBM)
PARAMS = pltpu.CompilerParams(vmem_limit_bytes=32 << 20)


def trig_table(length):
    n = np.arange(length)
    angles = (np.outer(n, n) % length) * (2.0 * np.pi / length)
    return np.cos(angles), np.sin(angles)


def make_tables():
    cos_x, sin_x = trig_table(NX)
    cos_z, sin_z = trig_table(NZ)
    table_x = np.concatenate([cos_x, -sin_x], axis=1)
    upper = np.concatenate([cos_z, -sin_z], axis=1)
    lower = np.concatenate([sin_z, cos_z], axis=1)
    table_z = np.concatenate([upper, lower], axis=0)
    table_z = table_z.reshape(2, N_SLAB, ZL, 2 * NZ).transpose(1, 0, 2, 3).reshape(2 * NZ, 2 * NZ)
    return jnp.asarray(table_x.astype(np.float32)).astype(BF), jnp.asarray(
        table_z.astype(np.float32)
    ).astype(BF)


def swap_chunks(parts):
    parts = list(parts)
    chunk = lax.broadcasted_iota(jnp.int32, parts[0].shape, 1) // KX
    for step in (1, 2, 4):
        upper = (chunk & step) != 0
        for i in range(8):
            if i & step:
                continue
            first, second = parts[i], parts[i | step]
            parts[i] = jnp.where(upper, pltpu.roll(second, step * KX, 1), first)
            parts[i | step] = jnp.where(upper, second, pltpu.roll(first, 128 - step * KX, 1))
    return parts


def encode_cells(cells, live):
    value = 1.0 + (cells & 127).astype(F32) * (1.0 / 128.0)
    for bit in range(6):
        value = value * jnp.where((cells >> (7 + bit)) & 1 == 1, F32(2.0 ** (1 << bit)), F32(1.0))
    value = value * jnp.where((cells >> 13) & 1 == 1, F32(1.0), F32(2.0**-64))
    return jnp.where(live, value, 0.0).astype(BF)


def decode_cells(code):
    value = code.astype(F32)
    live = value > 0.0
    top = value >= 1.0
    value = jnp.where(top, value, value * 2.0**64)
    high = jnp.where(top, 64, 0)
    for bit in range(5, -1, -1):
        over = value >= 2.0 ** (1 << bit)
        value = jnp.where(over, value * 2.0 ** -(1 << bit), value)
        high = high + jnp.where(over, 1 << bit, 0)
    low = ((value - 1.0) * 128.0).astype(jnp.int32)
    return jnp.where(live, high * 128 + low, -1)


def pack_kernel(
    tile_ref, live_ref, feat_hbm, cot_hbm, offset_ref, out_hbm, feat_ref, cot_ref, out_ref, sems
):
    size = C // PIECES
    copies = []
    for piece in range(PIECES):
        rows = pl.ds(piece * size, size)
        for n, (source, held) in enumerate(((feat_hbm, feat_ref), (cot_hbm, cot_ref))):
            copies.append(
                pltpu.make_async_copy(source.at[rows], held.at[rows], sems.at[2 * piece + n])
            )
    for copy in copies:
        copy.start()
    shape = (LT, 128)
    slot = lax.broadcasted_iota(jnp.int32, shape, 0) * 128 + lax.broadcasted_iota(
        jnp.int32, shape, 1
    )
    block = slot // BLK
    tile = jnp.zeros(shape, jnp.int32)
    for n in range(BLOCKS):
        tile = jnp.where(block == n, tile_ref[n], tile)
    offset = offset_ref[...]
    zy_cell = ((offset >> 3) & (NY - 1)) * ZL + (offset >> 5)
    cells = zy_cell * NX + tile * (NX // N_ROW) + (offset & 7)
    code = encode_cells(cells, slot < live_ref[0])
    for owner in range(N_ROW):
        out_ref[owner, LT] = code
    low = lax.broadcasted_iota(jnp.int32, (FC, 128), 0) < CL
    sent = []
    for piece in range(PIECES):
        copies[2 * piece].wait()
        copies[2 * piece + 1].wait()
        for pair in range(piece * size // FC, (piece + 1) * size // FC):
            rows = slice(pair * FC, (pair + 1) * FC)
            for j in range(LT):
                lanes = slice(j * 128, (j + 1) * 128)
                feat = feat_ref[rows, lanes].astype(F32)
                cot = cot_ref[rows, lanes].astype(F32)
                out_ref[2 * pair, j] = jnp.where(low, feat, pltpu.roll(cot, CL, 0)).astype(BF)
                out_ref[2 * pair + 1, j] = jnp.where(low, pltpu.roll(feat, CL, 0), cot).astype(BF)
        owners = pl.ds(piece * N_ROW // PIECES, N_ROW // PIECES)
        sent.append(
            pltpu.make_async_copy(
                out_ref.at[owners], out_hbm.at[owners], sems.at[2 * PIECES + piece]
            )
        )
        sent[-1].start()
    for copy in sent:
        copy.wait()


def pack(atom_feats, cotangent, block_tiles, cell_offsets, live_counts):
    return pl.pallas_call(
        pack_kernel,
        out_shape=jax.ShapeDtypeStruct((N_ROW, LT + 1, FC, 128), BF),
        in_specs=[SMEM, SMEM, HBM, HBM, VMEM],
        out_specs=HBM,
        scratch_shapes=[
            pltpu.VMEM((C, A_DEV), BF),
            pltpu.VMEM((C, A_DEV), BF),
            pltpu.VMEM((N_ROW, LT + 1, FC, 128), BF),
            pltpu.SemaphoreType.DMA((3 * PIECES,)),
        ],
        compiler_params=pltpu.CompilerParams(vmem_limit_bytes=60 * 1024 * 1024),
        name="pack",
    )(
        block_tiles.reshape(BLOCKS),
        live_counts,
        atom_feats,
        cotangent,
        cell_offsets.reshape(LT, 128),
    )


def unpack_kernel(in_ref, feat_hbm, cot_hbm, feat_ref, cot_ref, sems):
    low = lax.broadcasted_iota(jnp.int32, (FC, 128), 0) < CL
    size = C // PIECES
    sent = []
    for piece in range(PIECES):
        for pair in range(piece * size // FC, (piece + 1) * size // FC):
            rows = slice(pair * FC, (pair + 1) * FC)
            for j in range(LT):
                lanes = slice(j * 128, (j + 1) * 128)
                first = in_ref[2 * pair, j].astype(F32)
                second = in_ref[2 * pair + 1, j].astype(F32)
                feat_ref[rows, lanes] = jnp.where(low, first, pltpu.roll(second, CL, 0)).astype(BF)
                cot_ref[rows, lanes] = jnp.where(low, pltpu.roll(first, CL, 0), second).astype(BF)
        rows = pl.ds(piece * size, size)
        for n, (held, target) in enumerate(((feat_ref, feat_hbm), (cot_ref, cot_hbm))):
            sent.append(
                pltpu.make_async_copy(held.at[rows], target.at[rows], sems.at[2 * piece + n])
            )
            sent[-1].start()
    for copy in sent:
        copy.wait()


def unpack(values):
    shape = jax.ShapeDtypeStruct((C, A_DEV), BF)
    return pl.pallas_call(
        unpack_kernel,
        out_shape=(shape, shape),
        in_specs=[VMEM],
        out_specs=(HBM, HBM),
        scratch_shapes=[
            pltpu.VMEM((C, A_DEV), BF),
            pltpu.VMEM((C, A_DEV), BF),
            pltpu.SemaphoreType.DMA((2 * PIECES,)),
        ],
        compiler_params=PARAMS,
        name="unpack",
    )(values)


def on_rows(row, dtype):
    return jnp.broadcast_to(row, (PACK, 128)).astype(dtype)


def line_numbers(count, dtype):
    return [
        (lax.broadcasted_iota(jnp.int32, (PACK, 128), 0) + first).astype(F32).astype(dtype)
        for first in range(0, count, PACK)
    ]


def one_hot_x(x_row, lines):
    cell = on_rows(x_row, BF)
    one, zero = jnp.ones((PACK, 128), BF), jnp.zeros((PACK, 128), BF)
    return jnp.concatenate([jnp.where(cell == line, one, zero) for line in lines], axis=0)


def sum_rows(blocks):
    sub = lax.broadcasted_iota(jnp.int32, (8, 128), 0)
    low = (sub & 4) == 0
    blocks = [
        jnp.where(low, first, second) + pltpu.roll(jnp.where(low, second, first), 4, 0)
        for first, second in zip(blocks[:4], blocks[4:])
    ]
    for step in (2, 1):
        low = (sub & step) == 0
        blocks = [
            jnp.where(low, first + pltpu.roll(first, 8 - step, 0), second + pltpu.roll(second, step, 0))
            for first, second in zip(blocks[:step], blocks[step:])
        ]
    return blocks[0]


def spread_kernel(got_ref, table_ref, out_ref, list_ref, zy_ref, x_ref, acc_ref):
    first_lane = lax.broadcasted_iota(jnp.int32, (LT, 128), 1) == 0
    zy_ref[ROWS : ROWS + LT, :] = jnp.full((LT, 128), -1.0, F32)
    x_ref[ROWS : ROWS + LT, :] = jnp.zeros((LT, 128), F32)
    total = jnp.int32(0)
    for src in range(N_ROW):
        cells = decode_cells(got_ref[src, LT])
        rows = slice(src * LT, (src + 1) * LT)
        zy_ref[rows, :] = (cells >> 8).astype(F32)
        x_ref[rows, :] = (cells & (NX - 1)).astype(F32)
        live_rows = jnp.sum(jnp.where(first_lane & (cells >= 0), 1.0, 0.0)).astype(jnp.int32)
        for j in range(LT):
            list_ref[total + j] = src * LT + j
        total = total + live_rows
    for n in range(GROUP):
        list_ref[total + n] = ROWS
    steps = (total + GROUP - 1) // GROUP
    list_ref[LIST - 1] = steps

    acc_ref[...] = jnp.zeros_like(acc_ref)
    zero = jnp.zeros((PACK, 128), BF)

    def some_rows(step, carry):
        x_lines, zy_lines = line_numbers(NX, BF), line_numbers(ZY, BF)
        left, right = [], []
        for n in range(GROUP):
            row = list_ref[step * GROUP + n]
            held = jnp.minimum(row, ROWS - 1)
            values = got_ref[held // LT, held % LT].astype(F32)
            cell = on_rows(zy_ref[pl.ds(row, 1), :], BF)
            masks = [cell == line for line in zy_lines]
            right.append(one_hot_x(x_ref[pl.ds(row, 1), :], x_lines))
            parts = []
            for c in range(FC):
                value = on_rows(values[c : c + 1], BF)
                parts += [jnp.where(mask, value, zero) for mask in masks]
            left.append(jnp.concatenate(parts, axis=0))
        acc_ref[...] += lax.dot_general(
            jnp.concatenate(left, axis=1),
            jnp.concatenate(right, axis=1),
            NT,
            preferred_element_type=F32,
        )
        return carry

    lax.fori_loop(0, steps, some_rows, 0)
    for field in range(2):
        rows = jnp.dot(
            acc_ref[field * HALF : (field + 1) * HALF, :].astype(BF),
            table_ref[...],
            preferred_element_type=F32,
        )
        if field == 1:
            rows = rows * INV
        for part in range(2):
            for group in range(CL * NY // 8):
                for half in range(2):
                    lanes = part * NX + half * 128
                    chunks = swap_chunks(
                        [
                            rows[(group * 8 + i) * ZL : (group * 8 + i + 1) * ZL, lanes : lanes + 128]
                            for i in range(8)
                        ]
                    )
                    place = field * LINES + group * 128
                    for j in range(8):
                        out_ref[
                            half * 8 + j, part * ZL : (part + 1) * ZL, place : place + 128
                        ] = chunks[j].astype(BF)


def spread(got, table_x):
    cells = jax.ShapeDtypeStruct((ROWS + LT, 128), F32)
    return pl.pallas_call(
        spread_kernel,
        out_shape=(
            jax.ShapeDtypeStruct((N_SLAB, 2 * ZL, 2 * LINES), BF),
            jax.ShapeDtypeStruct((LIST,), jnp.int32),
            cells,
            cells,
        ),
        in_specs=[VMEM] * 2,
        out_specs=(VMEM, SMEM, VMEM, VMEM),
        scratch_shapes=[pltpu.VMEM((2 * HALF, NX), F32)],
        compiler_params=PARAMS,
        name="spread",
    )(got, table_x)


def spectral_kernel(cols_ref, table_ref, filter_ref, out_ref, grad_ref, mode_ref):
    table = table_ref[...]
    cols = cols_ref[...].reshape(2 * NZ, 2 * LINES)
    mode_ref[...] = lax.dot_general(cols, table, TN, preferred_element_type=F32).astype(BF)
    filtered, cot_spec = [], []
    for c in range(CL):
        filt = filter_ref[c * KX : (c + 1) * KX].astype(F32)
        fr, fi = filt[:, 0, :], filt[:, 1, :]
        grad_r = jnp.zeros((KX, NZ), F32)
        grad_i = jnp.zeros((KX, NZ), F32)
        for y in range(NY):
            first = (c * NY + y) * KX
            spec = mode_ref[first : first + KX, :].astype(F32)
            cot = mode_ref[LINES + first : LINES + first + KX, :].astype(F32)
            sr, si = spec[:, :NZ], spec[:, NZ:]
            gr, gi = cot[:, :NZ], cot[:, NZ:]
            filtered.append(jnp.concatenate([sr * fr - si * fi, sr * fi + si * fr], axis=1).astype(BF))
            cot_spec.append(jnp.concatenate([gr * fr + gi * fi, gi * fr - gr * fi], axis=1).astype(BF))
            grad_r = grad_r + (gr * sr + gi * si)
            grad_i = grad_i + (gi * sr - gr * si)
        grad_ref[c * KX : (c + 1) * KX, 0, :] = grad_r
        grad_ref[c * KX : (c + 1) * KX, 1, :] = grad_i
    for field, parts in enumerate((filtered, cot_spec)):
        planes = lax.dot_general(
            table, jnp.concatenate(parts, axis=0), NT, preferred_element_type=F32
        )
        out_ref[:, :, field * LINES : (field + 1) * LINES] = planes.astype(BF).reshape(
            N_SLAB, 2 * ZL, LINES
        )


def spectral(cols, table_z, filters):
    return pl.pallas_call(
        spectral_kernel,
        out_shape=(
            jax.ShapeDtypeStruct((N_SLAB, 2 * ZL, 2 * LINES), BF),
            jax.ShapeDtypeStruct((CL * KX, 2, NZ), F32),
        ),
        in_specs=[VMEM] * 3,
        out_specs=(VMEM,) * 2,
        scratch_shapes=[pltpu.VMEM((2 * LINES, 2 * NZ), BF)],
        compiler_params=PARAMS,
        name="spectral",
    )(cols, table_z, filters)


def gather_kernel(list_ref, plane_ref, table_ref, zy_ref, x_ref, out_ref, mode_ref, field_ref):
    for field in range(2):
        for part in range(2):
            for group in range(CL * NY // 8):
                place = field * LINES + group * 128
                for half in range(2):
                    chunks = swap_chunks(
                        [
                            plane_ref[
                                half * 8 + j, part * ZL : (part + 1) * ZL, place : place + 128
                            ].astype(F32)
                            for j in range(8)
                        ]
                    )
                    lanes = part * NX + half * 128
                    for i in range(8):
                        first = field * HALF + (group * 8 + i) * ZL
                        mode_ref[first : first + ZL, lanes : lanes + 128] = chunks[i].astype(BF)
    cells = lax.dot_general(mode_ref[...], table_ref[...], NT, preferred_element_type=F32)
    field_ref[:HALF, :] = (cells[:HALF] * INV).astype(BF)
    field_ref[HALF:, :] = cells[HALF:].astype(BF)
    out_ref[...] = jnp.zeros_like(out_ref)
    zy_line = lax.broadcasted_iota(jnp.int32, (8, 128), 0).astype(F32)

    def some_rows(step, carry):
        x_lines = line_numbers(NX, BF)
        for pair in range(0, GROUP, 2):
            rows = []
            for n in (pair, pair + 1):
                row = list_ref[step * GROUP + n]
                rows.append(jnp.where(row == ROWS, 0, row))
            picks = jnp.concatenate(
                [one_hot_x(x_ref[pl.ds(row, 1), :], x_lines) for row in rows], axis=1
            )
            lines = jnp.dot(field_ref[...], picks, preferred_element_type=F32)
            for n, row in enumerate(rows):
                cell = jnp.broadcast_to(zy_ref[pl.ds(row, 1), :], (8, 128))
                masks = [cell == zy_line + first for first in range(0, ZY, 8)]
                found = []
                for c in range(FC):
                    kept = jnp.zeros((8, 128), F32)
                    for k, mask in enumerate(masks):
                        first = c * ZY + k * 8
                        kept = jnp.where(
                            mask, lines[first : first + 8, n * 128 : (n + 1) * 128], kept
                        )
                    found.append(kept)
                out_ref[row // LT, row % LT] = sum_rows(found).astype(BF)
        return carry

    lax.fori_loop(0, list_ref[LIST - 1], some_rows, 0)


def gather(rows, planes, table_x, zy_cells, x_cells):
    return pl.pallas_call(
        gather_kernel,
        out_shape=jax.ShapeDtypeStruct((N_ROW, LT, FC, 128), BF),
        in_specs=[SMEM] + [VMEM] * 4,
        out_specs=VMEM,
        scratch_shapes=[pltpu.VMEM((2 * HALF, 2 * NX), BF), pltpu.VMEM((2 * HALF, NX), BF)],
        compiler_params=PARAMS,
        name="gather",
    )(rows, planes, table_x, zy_cells, x_cells)


def on_device(atom_feats, cotangent, filter_modes, block_tiles, cell_offsets, live_counts):
    table_x, table_z = make_tables()

    def over(axis, values):
        return lax.all_to_all(values, axis, split_axis=0, concat_axis=0, tiled=True)

    got = over("row", pack(atom_feats, cotangent, block_tiles, cell_offsets, live_counts))
    cols, rows, zy_cells, x_cells = spread(got, table_x)
    planes, grad = spectral(over("slab", cols), table_z, filter_modes.reshape(CL * KX, 2, NZ))
    found = gather(rows, over("slab", planes), table_x, zy_cells, x_cells)
    long_range, grad_feats = unpack(over("row", found))
    return (long_range, grad_feats, grad.reshape(CL, KX, 2, NZ))


def solution(mesh):
    in_specs = (
        P(None, ("slab", "row")),
        P(None, ("slab", "row")),
        P("row", "slab", None, None),
        P(("slab", "row"), None),
        P(("slab", "row")),
        P(("slab", "row")),
    )
    out_specs = (P(None, ("slab", "row")), P(None, ("slab", "row")), P("row", "slab", None, None))
    return jax.shard_map(
        on_device, mesh=mesh, in_specs=in_specs, out_specs=out_specs, check_vma=False
    )
```

```python
import jax
import jax.numpy as jnp
import numpy as np
from jax import lax
from jax.experimental import pallas as pl
from jax.experimental.pallas import tpu as pltpu
from jax.sharding import PartitionSpec as P

C = 128
NX = 256
NZ = 256
NY = 4
BLK = 32
N_SLAB = 16
N_ROW = 32
CL = C // N_ROW
FC = 2 * CL
KX = NX // N_SLAB
ZL = NZ // N_SLAB
A_DEV = 1024
LT = A_DEV // 128
BLOCKS = A_DEV // BLK
ZY = NY * ZL
HALF = CL * ZY
LINES = CL * NY * KX
INV = 1.0 / (NX * NZ)
PACK = 16
ROWS = N_ROW * LT
GROUP = 16
TILES = N_ROW
QUARTER = 4
PER_ROW = 128 // BLK
TALL = 2 * FC
PIECES = 4
LIST = ROWS + GROUP + LT
BF = jnp.bfloat16
F32 = jnp.float32
NT = (((1,), (1,)), ((), ()))
TN = (((0,), (0,)), ((), ()))
VMEM = pl.BlockSpec(memory_space=pltpu.VMEM)
SMEM = pl.BlockSpec(memory_space=pltpu.SMEM)
HBM = pl.BlockSpec(memory_space=pltpu.HBM)
PARAMS = pltpu.CompilerParams(vmem_limit_bytes=32 << 20)


def trig_table(length):
    n = np.arange(length)
    angles = (np.outer(n, n) % length) * (2.0 * np.pi / length)
    return np.cos(angles), np.sin(angles)


def make_tables():
    cos_x, sin_x = trig_table(NX)
    cos_z, sin_z = trig_table(NZ)
    table_x = np.concatenate([cos_x, -sin_x], axis=1)
    upper = np.concatenate([cos_z, -sin_z], axis=1)
    lower = np.concatenate([sin_z, cos_z], axis=1)
    table_z = np.concatenate([upper, lower], axis=0)
    table_x = table_x.reshape(TILES, 2, QUARTER, 2 * NX).transpose(2, 0, 1, 3).reshape(NX, 2 * NX)
    table_z = table_z.reshape(2, N_SLAB, ZL, 2 * NZ).transpose(1, 0, 2, 3).reshape(2 * NZ, 2 * NZ)
    return jnp.asarray(table_x.astype(np.float32)).astype(BF), jnp.asarray(
        table_z.astype(np.float32)
    ).astype(BF)


def swap_chunks(parts):
    parts = list(parts)
    chunk = lax.broadcasted_iota(jnp.int32, parts[0].shape, 1) // KX
    for step in (1, 2, 4):
        upper = (chunk & step) != 0
        for i in range(8):
            if i & step:
                continue
            first, second = parts[i], parts[i | step]
            parts[i] = jnp.where(upper, pltpu.roll(second, step * KX, 1), first)
            parts[i | step] = jnp.where(upper, second, pltpu.roll(first, 128 - step * KX, 1))
    return parts


def encode_cells(cells, live):
    value = 1.0 + (cells & 127).astype(F32) * (1.0 / 128.0)
    for bit in range(6):
        value = value * jnp.where((cells >> (7 + bit)) & 1 == 1, F32(2.0 ** (1 << bit)), F32(1.0))
    value = value * jnp.where((cells >> 13) & 1 == 1, F32(1.0), F32(2.0**-64))
    return jnp.where(live, value, 0.0).astype(BF)


def decode_cells(code):
    value = code.astype(F32)
    live = value > 0.0
    top = value >= 1.0
    value = jnp.where(top, value, value * 2.0**64)
    high = jnp.where(top, 64, 0)
    for bit in range(5, -1, -1):
        over = value >= 2.0 ** (1 << bit)
        value = jnp.where(over, value * 2.0 ** -(1 << bit), value)
        high = high + jnp.where(over, 1 << bit, 0)
    low = ((value - 1.0) * 128.0).astype(jnp.int32)
    return jnp.where(live, high * 128 + low, -1)


def pack_kernel(
    tile_ref, live_ref, feat_hbm, cot_hbm, offset_ref, out_hbm, feat_ref, cot_ref, out_ref, sems
):
    size = C // PIECES
    copies = []
    for piece in range(PIECES):
        rows = pl.ds(piece * size, size)
        for n, (source, held) in enumerate(((feat_hbm, feat_ref), (cot_hbm, cot_ref))):
            copies.append(
                pltpu.make_async_copy(source.at[rows], held.at[rows], sems.at[2 * piece + n])
            )
    for copy in copies:
        copy.start()
    shape = (LT, 128)
    slot = lax.broadcasted_iota(jnp.int32, shape, 0) * 128 + lax.broadcasted_iota(
        jnp.int32, shape, 1
    )
    block = slot // BLK
    tile = jnp.zeros(shape, jnp.int32)
    for n in range(BLOCKS):
        tile = jnp.where(block == n, tile_ref[n], tile)
    offset = offset_ref[...]
    zy_cell = ((offset >> 3) & (NY - 1)) * ZL + (offset >> 5)
    cells = zy_cell * NX + tile * (NX // N_ROW) + (offset & 7)
    code = encode_cells(cells, slot < live_ref[0])
    for owner in range(N_ROW):
        out_ref[owner, LT] = code
    low = lax.broadcasted_iota(jnp.int32, (FC, 128), 0) < CL
    sent = []
    for piece in range(PIECES):
        copies[2 * piece].wait()
        copies[2 * piece + 1].wait()
        for pair in range(piece * size // FC, (piece + 1) * size // FC):
            rows = slice(pair * FC, (pair + 1) * FC)
            for j in range(LT):
                lanes = slice(j * 128, (j + 1) * 128)
                feat = feat_ref[rows, lanes].astype(F32)
                cot = cot_ref[rows, lanes].astype(F32)
                out_ref[2 * pair, j] = jnp.where(low, feat, pltpu.roll(cot, CL, 0)).astype(BF)
                out_ref[2 * pair + 1, j] = jnp.where(low, pltpu.roll(feat, CL, 0), cot).astype(BF)
        owners = pl.ds(piece * N_ROW // PIECES, N_ROW // PIECES)
        sent.append(
            pltpu.make_async_copy(
                out_ref.at[owners], out_hbm.at[owners], sems.at[2 * PIECES + piece]
            )
        )
        sent[-1].start()
    for copy in sent:
        copy.wait()


def pack(atom_feats, cotangent, block_tiles, cell_offsets, live_counts):
    return pl.pallas_call(
        pack_kernel,
        out_shape=jax.ShapeDtypeStruct((N_ROW, LT + 1, FC, 128), BF),
        in_specs=[SMEM, SMEM, HBM, HBM, VMEM],
        out_specs=HBM,
        scratch_shapes=[
            pltpu.VMEM((C, A_DEV), BF),
            pltpu.VMEM((C, A_DEV), BF),
            pltpu.VMEM((N_ROW, LT + 1, FC, 128), BF),
            pltpu.SemaphoreType.DMA((3 * PIECES,)),
        ],
        compiler_params=pltpu.CompilerParams(vmem_limit_bytes=60 * 1024 * 1024),
        name="pack",
    )(
        block_tiles.reshape(BLOCKS),
        live_counts,
        atom_feats,
        cotangent,
        cell_offsets.reshape(LT, 128),
    )


def unpack_kernel(in_ref, feat_hbm, cot_hbm, feat_ref, cot_ref, sems):
    low = lax.broadcasted_iota(jnp.int32, (FC, 128), 0) < CL
    size = C // PIECES
    sent = []
    for piece in range(PIECES):
        for pair in range(piece * size // FC, (piece + 1) * size // FC):
            rows = slice(pair * FC, (pair + 1) * FC)
            for j in range(LT):
                lanes = slice(j * 128, (j + 1) * 128)
                first = in_ref[2 * pair, j].astype(F32)
                second = in_ref[2 * pair + 1, j].astype(F32)
                feat_ref[rows, lanes] = jnp.where(low, first, pltpu.roll(second, CL, 0)).astype(BF)
                cot_ref[rows, lanes] = jnp.where(low, pltpu.roll(first, CL, 0), second).astype(BF)
        rows = pl.ds(piece * size, size)
        for n, (held, target) in enumerate(((feat_ref, feat_hbm), (cot_ref, cot_hbm))):
            sent.append(
                pltpu.make_async_copy(held.at[rows], target.at[rows], sems.at[2 * piece + n])
            )
            sent[-1].start()
    for copy in sent:
        copy.wait()


def unpack(values):
    shape = jax.ShapeDtypeStruct((C, A_DEV), BF)
    return pl.pallas_call(
        unpack_kernel,
        out_shape=(shape, shape),
        in_specs=[VMEM],
        out_specs=(HBM, HBM),
        scratch_shapes=[
            pltpu.VMEM((C, A_DEV), BF),
            pltpu.VMEM((C, A_DEV), BF),
            pltpu.SemaphoreType.DMA((2 * PIECES,)),
        ],
        compiler_params=PARAMS,
        name="unpack",
    )(values)


def line_numbers(count, dtype):
    return [
        (lax.broadcasted_iota(jnp.int32, (PACK, 128), 0) + first).astype(F32).astype(dtype)
        for first in range(0, count, PACK)
    ]


def one_hot(row, lines):
    cell = jnp.broadcast_to(row, (PACK, 128)).astype(BF)
    one, zero = jnp.ones((PACK, 128), BF), jnp.zeros((PACK, 128), BF)
    return jnp.concatenate([jnp.where(cell == line, one, zero) for line in lines], axis=0)


def swap_halves(first, second):
    low = lax.broadcasted_iota(jnp.int32, first.shape, 1) < 64
    return (
        jnp.where(low, first, pltpu.roll(second, 64, 1)),
        jnp.where(low, pltpu.roll(first, 64, 1), second),
    )


def tile_rows(info_ref, row):
    info = info_ref[row & (LT - 1), row >> 3]
    return [
        pl.multiple_of((info >> (5 * k)) & ((TILES - 1) * TALL), TALL) for k in range(PER_ROW)
    ]


def spread_kernel(
    got_ref, table_ref, out_ref, list_ref, info_ref, cell_ref, half_ref, held_ref, sem, mesh_ref, *accs
):
    lane = lax.broadcasted_iota(jnp.int32, (LT, 128), 1)
    cell_ref[ROWS : ROWS + LT, :] = jnp.full((LT, 128), -1.0, F32)
    half_ref[ROWS : ROWS + LT, :] = jnp.zeros((LT, 128), F32)
    infos = jnp.zeros((LT, 128), F32)
    for src in range(N_ROW):
        cells = decode_cells(got_ref[src, LT])
        live = cells >= 0
        rows = slice(src * LT, (src + 1) * LT)
        x_cell = cells & (NX - 1)
        cell_ref[rows, :] = jnp.where(
            live, (x_cell & (QUARTER - 1)) * ZY + (cells >> 8), -1
        ).astype(F32)
        half_ref[rows, :] = ((x_cell >> 2) & 1).astype(F32)
        tile = ((x_cell >> 3) * TALL) << (5 * (lane // BLK))
        tiles = jnp.sum(
            jnp.where(live & (lane % BLK == 0), tile, 0).astype(F32), axis=1, keepdims=True
        )
        count = jnp.sum(jnp.where(live & (lane == 0), 1.0, 0.0), keepdims=True)
        infos = jnp.where(lane == src, jnp.broadcast_to(tiles, (LT, 128)), infos)
        infos = jnp.where(lane == 64 + src, jnp.broadcast_to(count, (LT, 128)), infos)
    held_ref[...] = infos.astype(jnp.int32)
    copy = pltpu.make_async_copy(held_ref, info_ref, sem)
    copy.start()
    for acc in accs:
        acc[...] = jnp.zeros_like(acc)
    copy.wait()
    total = jnp.int32(0)
    for src in range(N_ROW):
        for j in range(LT):
            list_ref[total + j] = src * LT + j
        total = total + info_ref[0, 64 + src]
    for n in range(GROUP):
        list_ref[total + n] = ROWS
    steps = (total + GROUP - 1) // GROUP
    list_ref[LIST - 1] = steps

    zero = jnp.zeros((TALL, 128), BF)
    upper = (lax.broadcasted_iota(jnp.int32, (TALL, 128), 0) // FC).astype(F32).astype(BF)
    block = (lax.broadcasted_iota(jnp.int32, (TALL, 128), 1) // BLK).astype(F32).astype(BF)

    def some_rows(step, carry):
        lines = line_numbers(NX, BF)
        for pair in range(0, GROUP, 2):
            right, left, places = [], [], []
            for n in range(2):
                row = list_ref[step * GROUP + pair + n]
                held = jnp.minimum(row, ROWS - 1)
                values = got_ref[held >> 3, held & (LT - 1)].astype(F32)
                half = jnp.broadcast_to(half_ref[pl.ds(row, 1), :], (TALL, 128)).astype(BF)
                values = jnp.where(
                    half == upper, jnp.concatenate([values, values], axis=0).astype(BF), zero
                )
                right.append(one_hot(cell_ref[pl.ds(row, 1), :], lines))
                mine = [jnp.where(block == float(k), values, zero) for k in range(PER_ROW)]
                none = [zero] * PER_ROW
                left.append(jnp.concatenate(mine + none if n == 0 else none + mine, axis=0))
                places += tile_rows(info_ref, row)
            sums = lax.dot_general(
                jnp.concatenate(left, axis=1),
                jnp.concatenate(right, axis=1),
                NT,
                preferred_element_type=F32,
            )
            for k, place in enumerate(places):
                for col in range(2):
                    acc = accs[2 * (k % PER_ROW) + col]
                    acc[pl.ds(place, TALL), :] += sums[
                        k * TALL : (k + 1) * TALL, col * 128 : (col + 1) * 128
                    ]
        return carry

    lax.fori_loop(0, steps, some_rows, 0)
    for col in range(2):
        accs[col][...] += accs[2 + col][...] + accs[4 + col][...] + accs[6 + col][...]
    for pair in range(FC // 2):
        for col in range(2):
            even, odd = (
                accs[col][pl.ds(2 * pair + n, 2 * TILES, stride=FC), :]
                for n in range(2)
            )
            for n, block_rows in enumerate(swap_halves(even, odd)):
                first = (2 * col + n) * 2 * TILES
                mesh_ref[first : first + 2 * TILES, pair * 128 : (pair + 1) * 128] = (
                    block_rows.astype(BF)
                )
    for field in range(2):
        rows = lax.dot_general(
            mesh_ref[:, field * HALF : (field + 1) * HALF],
            table_ref[...],
            TN,
            preferred_element_type=F32,
        )
        rows = (rows * INV if field == 1 else rows).astype(BF)
        for part in range(2):
            for group in range(CL * NY // 8):
                for half in range(2):
                    lanes = part * NX + half * 128
                    chunks = swap_chunks(
                        [
                            rows[(group * 8 + i) * ZL : (group * 8 + i + 1) * ZL, lanes : lanes + 128]
                            for i in range(8)
                        ]
                    )
                    place = field * LINES + group * 128
                    for j in range(8):
                        out_ref[
                            half * 8 + j, part * ZL : (part + 1) * ZL, place : place + 128
                        ] = chunks[j]


def spread(got, table_x):
    cells = jax.ShapeDtypeStruct((ROWS + LT, 128), F32)
    return pl.pallas_call(
        spread_kernel,
        out_shape=(
            jax.ShapeDtypeStruct((N_SLAB, 2 * ZL, 2 * LINES), BF),
            jax.ShapeDtypeStruct((LIST,), jnp.int32),
            jax.ShapeDtypeStruct((LT, 128), jnp.int32),
            cells,
            cells,
        ),
        in_specs=[VMEM] * 2,
        out_specs=(VMEM, SMEM, SMEM, VMEM, VMEM),
        scratch_shapes=[
            pltpu.VMEM((LT, 128), jnp.int32),
            pltpu.SemaphoreType.DMA(()),
            pltpu.VMEM((NX, 2 * HALF), BF),
        ]
        + [pltpu.VMEM((TILES * TALL, 128), F32)] * (2 * PER_ROW),
        compiler_params=PARAMS,
        name="spread",
    )(got, table_x)


def spectral_kernel(cols_ref, table_ref, filter_ref, out_ref, grad_ref, mode_ref):
    table = table_ref[...]
    cols = cols_ref[...].reshape(2 * NZ, 2 * LINES)
    mode_ref[...] = lax.dot_general(cols, table, TN, preferred_element_type=F32).astype(BF)
    filtered, cot_spec = [], []
    for c in range(CL):
        filt = filter_ref[c * KX : (c + 1) * KX].astype(F32)
        fr, fi = filt[:, 0, :], filt[:, 1, :]
        grad_r = jnp.zeros((KX, NZ), F32)
        grad_i = jnp.zeros((KX, NZ), F32)
        for y in range(NY):
            first = (c * NY + y) * KX
            spec = mode_ref[first : first + KX, :].astype(F32)
            cot = mode_ref[LINES + first : LINES + first + KX, :].astype(F32)
            sr, si = spec[:, :NZ], spec[:, NZ:]
            gr, gi = cot[:, :NZ], cot[:, NZ:]
            filtered.append(jnp.concatenate([sr * fr - si * fi, sr * fi + si * fr], axis=1).astype(BF))
            cot_spec.append(jnp.concatenate([gr * fr + gi * fi, gi * fr - gr * fi], axis=1).astype(BF))
            grad_r = grad_r + (gr * sr + gi * si)
            grad_i = grad_i + (gi * sr - gr * si)
        grad_ref[c * KX : (c + 1) * KX, 0, :] = grad_r
        grad_ref[c * KX : (c + 1) * KX, 1, :] = grad_i
    for field, parts in enumerate((filtered, cot_spec)):
        planes = lax.dot_general(
            table, jnp.concatenate(parts, axis=0), NT, preferred_element_type=F32
        )
        out_ref[:, :, field * LINES : (field + 1) * LINES] = planes.astype(BF).reshape(
            N_SLAB, 2 * ZL, LINES
        )


def spectral(cols, table_z, filters):
    return pl.pallas_call(
        spectral_kernel,
        out_shape=(
            jax.ShapeDtypeStruct((N_SLAB, 2 * ZL, 2 * LINES), BF),
            jax.ShapeDtypeStruct((CL * KX, 2, NZ), F32),
        ),
        in_specs=[VMEM] * 3,
        out_specs=(VMEM,) * 2,
        scratch_shapes=[pltpu.VMEM((2 * LINES, 2 * NZ), BF)],
        compiler_params=PARAMS,
        name="spectral",
    )(cols, table_z, filters)


def gather_kernel(
    list_ref, info_ref, plane_ref, table_ref, cell_ref, half_ref, out_ref, mode_ref, field_ref, *wide_refs
):
    for field in range(2):
        for part in range(2):
            for group in range(CL * NY // 8):
                place = field * LINES + group * 128
                for half in range(2):
                    chunks = swap_chunks(
                        [
                            plane_ref[
                                half * 8 + j, part * ZL : (part + 1) * ZL, place : place + 128
                            ]
                            for j in range(8)
                        ]
                    )
                    lanes = part * NX + half * 128
                    for i in range(8):
                        first = field * HALF + (group * 8 + i) * ZL
                        mode_ref[first : first + ZL, lanes : lanes + 128] = chunks[i]
    for field in range(2):
        cells = lax.dot_general(
            table_ref[...],
            mode_ref[field * HALF : (field + 1) * HALF, :],
            NT,
            preferred_element_type=F32,
        )
        if field == 0:
            cells = cells * INV
        for pair in range(CL // 2):
            lanes = slice(pair * 128, (pair + 1) * 128)
            for col in range(2):
                first = 2 * col * 2 * TILES
                swapped = swap_halves(
                    cells[first : first + 2 * TILES, lanes],
                    cells[first + 2 * TILES : first + 4 * TILES, lanes],
                )
                for n in range(2):
                    wide_refs[col][
                        pl.ds(field * CL + 2 * pair + n, 2 * TILES, stride=FC), :
                    ] = swapped[n]
    for col in range(2):
        field_ref[:, col * 128 : (col + 1) * 128] = wide_refs[col][...].astype(BF)
    out_ref[...] = jnp.zeros_like(out_ref)
    block = 2.0 * (lax.broadcasted_iota(jnp.int32, (FC, 128), 1) // BLK).astype(F32)

    def some_rows(step, carry):
        lines = line_numbers(NX, BF)
        for pair in range(0, GROUP, 2):
            rows, places, picks = [], [], []
            for n in range(2):
                row = list_ref[step * GROUP + pair + n]
                row = jnp.where(row == ROWS, 0, row)
                rows.append(row)
                places += tile_rows(info_ref, row)
                picks.append(one_hot(cell_ref[pl.ds(row, 1), :], lines))
            found = jnp.dot(
                jnp.concatenate([field_ref[pl.ds(place, TALL), :] for place in places], axis=0),
                jnp.concatenate(picks, axis=1),
                preferred_element_type=F32,
            )
            for n, row in enumerate(rows):
                wanted = block + jnp.broadcast_to(half_ref[pl.ds(row, 1), :], (FC, 128))
                kept = jnp.zeros((FC, 128), F32)
                for k in range(2 * PER_ROW):
                    first = n * PER_ROW * TALL + k * FC
                    kept = jnp.where(
                        wanted == float(k),
                        found[first : first + FC, n * 128 : (n + 1) * 128],
                        kept,
                    )
                out_ref[row >> 3, row & (LT - 1)] = kept.astype(BF)
        return carry

    lax.fori_loop(0, list_ref[LIST - 1], some_rows, 0)


def gather(rows, infos, planes, table_x, cells, halves):
    return pl.pallas_call(
        gather_kernel,
        out_shape=jax.ShapeDtypeStruct((N_ROW, LT, FC, 128), BF),
        in_specs=[SMEM] * 2 + [VMEM] * 4,
        out_specs=VMEM,
        scratch_shapes=[
            pltpu.VMEM((2 * HALF, 2 * NX), BF),
            pltpu.VMEM((TILES * TALL, NX), BF),
            pltpu.VMEM((TILES * TALL, 128), F32),
            pltpu.VMEM((TILES * TALL, 128), F32),
        ],
        compiler_params=PARAMS,
        name="gather",
    )(rows, infos, planes, table_x, cells, halves)


def on_device(atom_feats, cotangent, filter_modes, block_tiles, cell_offsets, live_counts):
    table_x, table_z = make_tables()

    def over(axis, values):
        return lax.all_to_all(values, axis, split_axis=0, concat_axis=0, tiled=True)

    got = over("row", pack(atom_feats, cotangent, block_tiles, cell_offsets, live_counts))
    cols, rows, infos, cells, halves = spread(got, table_x)
    planes, grad = spectral(over("slab", cols), table_z, filter_modes.reshape(CL * KX, 2, NZ))
    found = gather(rows, infos, over("slab", planes), table_x, cells, halves)
    long_range, grad_feats = unpack(over("row", found))
    return (long_range, grad_feats, grad.reshape(CL, KX, 2, NZ))


def solution(mesh):
    in_specs = (
        P(None, ("slab", "row")),
        P(None, ("slab", "row")),
        P("row", "slab", None, None),
        P(("slab", "row"), None),
        P(("slab", "row")),
        P(("slab", "row")),
    )
    out_specs = (P(None, ("slab", "row")), P(None, ("slab", "row")), P("row", "slab", None, None))
    return jax.shard_map(
        on_device, mesh=mesh, in_specs=in_specs, out_specs=out_specs, check_vma=False
    )
```

```python
import jax
import jax.numpy as jnp
import numpy as np
from jax import lax
from jax.experimental import pallas as pl
from jax.experimental.pallas import tpu as pltpu
from jax.sharding import PartitionSpec as P

C = 128
NX = 256
NZ = 256
NY = 4
BLK = 32
N_SLAB = 16
N_ROW = 32
CL = C // N_ROW
FC = 2 * CL
KX = NX // N_SLAB
ZL = NZ // N_SLAB
A_DEV = 1024
LT = A_DEV // 128
BLOCKS = A_DEV // BLK
ZY = NY * ZL
HALF = CL * ZY
LINES = CL * NY * KX
INV = 1.0 / (NX * NZ)
PACK = 16
ROWS = N_ROW * LT
GROUP = 32
TILES = N_ROW
QUARTER = 4
PER_ROW = 128 // BLK
TALL = 2 * FC
SETS = 2
PIECES = 4
LIST = ROWS + GROUP + LT
BF = jnp.bfloat16
F32 = jnp.float32
NT = (((1,), (1,)), ((), ()))
TN = (((0,), (0,)), ((), ()))
VMEM = pl.BlockSpec(memory_space=pltpu.VMEM)
SMEM = pl.BlockSpec(memory_space=pltpu.SMEM)
HBM = pl.BlockSpec(memory_space=pltpu.HBM)
PARAMS = pltpu.CompilerParams(vmem_limit_bytes=32 << 20)


def trig_table(length):
    n = np.arange(length)
    angles = (np.outer(n, n) % length) * (2.0 * np.pi / length)
    return np.cos(angles), np.sin(angles)


def make_tables():
    cos_x, sin_x = trig_table(NX)
    cos_z, sin_z = trig_table(NZ)
    table_x = np.concatenate([cos_x, -sin_x], axis=1)
    upper = np.concatenate([cos_z, -sin_z], axis=1)
    lower = np.concatenate([sin_z, cos_z], axis=1)
    table_z = np.concatenate([upper, lower], axis=0)
    table_x = table_x.reshape(TILES, 2, QUARTER, 2 * NX).transpose(2, 0, 1, 3).reshape(NX, 2 * NX)
    table_z = table_z.reshape(2, N_SLAB, ZL, 2 * NZ).transpose(1, 0, 2, 3).reshape(2 * NZ, 2 * NZ)
    return jnp.asarray(table_x.astype(np.float32)).astype(BF), jnp.asarray(
        table_z.astype(np.float32)
    ).astype(BF)


def swap_chunks(parts):
    parts = list(parts)
    chunk = lax.broadcasted_iota(jnp.int32, parts[0].shape, 1) // KX
    for step in (1, 2, 4):
        upper = (chunk & step) != 0
        for i in range(8):
            if i & step:
                continue
            first, second = parts[i], parts[i | step]
            parts[i] = jnp.where(upper, pltpu.roll(second, step * KX, 1), first)
            parts[i | step] = jnp.where(upper, second, pltpu.roll(first, 128 - step * KX, 1))
    return parts


def encode_cells(cells, live):
    value = 1.0 + (cells & 127).astype(F32) * (1.0 / 128.0)
    for bit in range(6):
        value = value * jnp.where((cells >> (7 + bit)) & 1 == 1, F32(2.0 ** (1 << bit)), F32(1.0))
    value = value * jnp.where((cells >> 13) & 1 == 1, F32(1.0), F32(2.0**-64))
    return jnp.where(live, value, 0.0).astype(BF)


def decode_cells(code):
    value = code.astype(F32)
    live = value > 0.0
    top = value >= 1.0
    value = jnp.where(top, value, value * 2.0**64)
    high = jnp.where(top, 64, 0)
    for bit in range(5, -1, -1):
        over = value >= 2.0 ** (1 << bit)
        value = jnp.where(over, value * 2.0 ** -(1 << bit), value)
        high = high + jnp.where(over, 1 << bit, 0)
    low = ((value - 1.0) * 128.0).astype(jnp.int32)
    return jnp.where(live, high * 128 + low, -1)


def pack_kernel(
    tile_hbm, live_hbm, feat_hbm, cot_hbm, offset_hbm, out_hbm,
    tile_ref, live_ref, feat_ref, cot_ref, offset_ref, out_ref, sems,
):
    size = C // PIECES
    small = [
        pltpu.make_async_copy(source, held, sems.at[3 * PIECES + n])
        for n, (source, held) in enumerate(
            ((tile_hbm, tile_ref), (live_hbm, live_ref), (offset_hbm, offset_ref))
        )
    ]
    copies = []
    for piece in range(PIECES):
        rows = pl.ds(piece * size, size)
        for n, (source, held) in enumerate(((feat_hbm, feat_ref), (cot_hbm, cot_ref))):
            copies.append(
                pltpu.make_async_copy(source.at[rows], held.at[rows], sems.at[2 * piece + n])
            )
    for copy in small + copies:
        copy.start()
    for copy in small:
        copy.wait()
    shape = (LT, 128)
    slot = lax.broadcasted_iota(jnp.int32, shape, 0) * 128 + lax.broadcasted_iota(
        jnp.int32, shape, 1
    )
    block = slot // BLK
    tile = jnp.zeros(shape, jnp.int32)
    for n in range(BLOCKS):
        tile = jnp.where(block == n, tile_ref[n], tile)
    offset = offset_ref[...]
    zy_cell = ((offset >> 3) & (NY - 1)) * ZL + (offset >> 5)
    cells = zy_cell * NX + tile * (NX // N_ROW) + (offset & 7)
    code = encode_cells(cells, slot < live_ref[0, 0])
    for owner in range(N_ROW):
        out_ref[owner, LT] = code
    low = lax.broadcasted_iota(jnp.int32, (FC, 128), 0) < CL
    sent = []
    for piece in range(PIECES):
        copies[2 * piece].wait()
        copies[2 * piece + 1].wait()
        for pair in range(piece * size // FC, (piece + 1) * size // FC):
            rows = slice(pair * FC, (pair + 1) * FC)
            for j in range(LT):
                lanes = slice(j * 128, (j + 1) * 128)
                feat = feat_ref[rows, lanes].astype(F32)
                cot = cot_ref[rows, lanes].astype(F32)
                out_ref[2 * pair, j] = jnp.where(low, feat, pltpu.roll(cot, CL, 0)).astype(BF)
                out_ref[2 * pair + 1, j] = jnp.where(low, pltpu.roll(feat, CL, 0), cot).astype(BF)
        owners = pl.ds(piece * N_ROW // PIECES, N_ROW // PIECES)
        sent.append(
            pltpu.make_async_copy(
                out_ref.at[owners], out_hbm.at[owners], sems.at[2 * PIECES + piece]
            )
        )
        sent[-1].start()
    for copy in sent:
        copy.wait()


def pack(atom_feats, cotangent, block_tiles, cell_offsets, live_counts):
    return pl.pallas_call(
        pack_kernel,
        out_shape=jax.ShapeDtypeStruct((N_ROW, LT + 1, FC, 128), BF),
        in_specs=[HBM] * 5,
        out_specs=HBM,
        scratch_shapes=[
            pltpu.SMEM((BLOCKS,), jnp.int32),
            pltpu.SMEM((1, 1), jnp.int32),
            pltpu.VMEM((C, A_DEV), BF),
            pltpu.VMEM((C, A_DEV), BF),
            pltpu.VMEM((LT, 128), jnp.int32),
            pltpu.VMEM((N_ROW, LT + 1, FC, 128), BF),
            pltpu.SemaphoreType.DMA((3 * PIECES + 3,)),
        ],
        compiler_params=pltpu.CompilerParams(vmem_limit_bytes=60 * 1024 * 1024),
        name="pack",
    )(
        block_tiles.reshape(BLOCKS),
        live_counts.reshape(1, 1),
        atom_feats,
        cotangent,
        cell_offsets.reshape(LT, 128),
    )


def unpack_kernel(in_ref, feat_hbm, cot_hbm, feat_ref, cot_ref, sems):
    low = lax.broadcasted_iota(jnp.int32, (FC, 128), 0) < CL
    size = C // PIECES
    sent = []
    for piece in range(PIECES):
        for pair in range(piece * size // FC, (piece + 1) * size // FC):
            rows = slice(pair * FC, (pair + 1) * FC)
            for j in range(LT):
                lanes = slice(j * 128, (j + 1) * 128)
                first = in_ref[2 * pair, j].astype(F32)
                second = in_ref[2 * pair + 1, j].astype(F32)
                feat_ref[rows, lanes] = jnp.where(low, first, pltpu.roll(second, CL, 0)).astype(BF)
                cot_ref[rows, lanes] = jnp.where(low, pltpu.roll(first, CL, 0), second).astype(BF)
        rows = pl.ds(piece * size, size)
        for n, (held, target) in enumerate(((feat_ref, feat_hbm), (cot_ref, cot_hbm))):
            sent.append(
                pltpu.make_async_copy(held.at[rows], target.at[rows], sems.at[2 * piece + n])
            )
            sent[-1].start()
    for copy in sent:
        copy.wait()


def unpack(values):
    shape = jax.ShapeDtypeStruct((C, A_DEV), BF)
    return pl.pallas_call(
        unpack_kernel,
        out_shape=(shape, shape),
        in_specs=[VMEM],
        out_specs=(HBM, HBM),
        scratch_shapes=[
            pltpu.VMEM((C, A_DEV), BF),
            pltpu.VMEM((C, A_DEV), BF),
            pltpu.SemaphoreType.DMA((2 * PIECES,)),
        ],
        compiler_params=PARAMS,
        name="unpack",
    )(values)


def line_numbers(count, dtype):
    return [
        (lax.broadcasted_iota(jnp.int32, (PACK, 128), 0) + first).astype(F32).astype(dtype)
        for first in range(0, count, PACK)
    ]


def one_hot(row, lines):
    cell = jnp.broadcast_to(row, (PACK, 128)).astype(BF)
    one, zero = jnp.ones((PACK, 128), BF), jnp.zeros((PACK, 128), BF)
    return jnp.concatenate([jnp.where(cell == line, one, zero) for line in lines], axis=0)


def swap_halves(first, second):
    low = lax.broadcasted_iota(jnp.int32, first.shape, 1) < 64
    return (
        jnp.where(low, first, pltpu.roll(second, 64, 1)),
        jnp.where(low, pltpu.roll(first, 64, 1), second),
    )


def tile_rows(info_ref, row):
    info = info_ref[row & (LT - 1), row >> 3]
    return [
        pl.multiple_of((info >> (5 * k)) & ((TILES - 1) * TALL), TALL) for k in range(PER_ROW)
    ]


def spread_kernel(
    got_ref, table_ref, out_ref, list_ref, info_ref, cell_ref, half_ref, held_ref, sem, mesh_ref, *accs
):
    lane = lax.broadcasted_iota(jnp.int32, (LT, 128), 1)
    cell_ref[ROWS : ROWS + LT, :] = jnp.full((LT, 128), -1.0, F32)
    half_ref[ROWS : ROWS + LT, :] = jnp.zeros((LT, 128), F32)
    infos = jnp.zeros((LT, 128), F32)
    total = jnp.int32(0)
    for src in range(N_ROW):
        cells = decode_cells(got_ref[src, LT])
        live = cells >= 0
        rows = slice(src * LT, (src + 1) * LT)
        x_cell = cells & (NX - 1)
        cell_ref[rows, :] = jnp.where(
            live, (x_cell & (QUARTER - 1)) * ZY + (cells >> 8), -1
        ).astype(F32)
        half_ref[rows, :] = ((x_cell >> 2) & 1).astype(F32)
        tile = ((x_cell >> 3) * TALL) << (5 * (lane // BLK))
        tiles = jnp.sum(
            jnp.where(live & (lane % BLK == 0), tile, 0).astype(F32), axis=1, keepdims=True
        )
        for j in range(LT):
            list_ref[total + j] = src * LT + j
        total = total + jnp.sum(jnp.where(live & (lane == 0), 1.0, 0.0)).astype(jnp.int32)
        infos = jnp.where(lane == src, jnp.broadcast_to(tiles, (LT, 128)), infos)
    held_ref[...] = infos.astype(jnp.int32)
    copy = pltpu.make_async_copy(held_ref, info_ref, sem)
    copy.start()
    for acc in accs:
        acc[...] = jnp.zeros_like(acc)
    copy.wait()
    for n in range(GROUP):
        list_ref[total + n] = ROWS
    steps = (total + GROUP - 1) // GROUP
    list_ref[LIST - 1] = steps

    zero = jnp.zeros((TALL, 128), BF)
    upper = (lax.broadcasted_iota(jnp.int32, (TALL, 128), 0) // FC).astype(F32).astype(BF)
    block = (lax.broadcasted_iota(jnp.int32, (TALL, 128), 1) // BLK).astype(F32).astype(BF)

    def some_rows(step, carry):
        lines = line_numbers(NX, BF)
        for pair in range(0, GROUP, 2):
            right, left, places = [], [], []
            for n in range(2):
                row = list_ref[step * GROUP + pair + n]
                held = jnp.minimum(row, ROWS - 1)
                values = got_ref[held >> 3, held & (LT - 1)].astype(F32)
                half = jnp.broadcast_to(half_ref[pl.ds(row, 1), :], (TALL, 128)).astype(BF)
                values = jnp.where(
                    half == upper, jnp.concatenate([values, values], axis=0).astype(BF), zero
                )
                right.append(one_hot(cell_ref[pl.ds(row, 1), :], lines))
                mine = [jnp.where(block == float(k), values, zero) for k in range(PER_ROW)]
                none = [zero] * PER_ROW
                left.append(jnp.concatenate(mine + none if n == 0 else none + mine, axis=0))
                places += tile_rows(info_ref, row)
            sums = lax.dot_general(
                jnp.concatenate(left, axis=1),
                jnp.concatenate(right, axis=1),
                NT,
                preferred_element_type=F32,
            )
            for k, place in enumerate(places):
                for col in range(2):
                    acc = accs[2 * (k % SETS) + col]
                    acc[pl.ds(place, TALL), :] += sums[
                        k * TALL : (k + 1) * TALL, col * 128 : (col + 1) * 128
                    ]
        return carry

    lax.fori_loop(0, steps, some_rows, 0)
    for col in range(2):
        accs[col][...] += accs[2 + col][...]
    for pair in range(FC // 2):
        for col in range(2):
            even, odd = (
                accs[col][pl.ds(2 * pair + n, 2 * TILES, stride=FC), :]
                for n in range(2)
            )
            for n, block_rows in enumerate(swap_halves(even, odd)):
                first = (2 * col + n) * 2 * TILES
                mesh_ref[first : first + 2 * TILES, pair * 128 : (pair + 1) * 128] = (
                    block_rows.astype(BF)
                )
    for field in range(2):
        rows = lax.dot_general(
            mesh_ref[:, field * HALF : (field + 1) * HALF],
            table_ref[...],
            TN,
            preferred_element_type=F32,
        )
        rows = (rows * INV if field == 1 else rows).astype(BF)
        for part in range(2):
            for group in range(CL * NY // 8):
                for half in range(2):
                    lanes = part * NX + half * 128
                    chunks = swap_chunks(
                        [
                            rows[(group * 8 + i) * ZL : (group * 8 + i + 1) * ZL, lanes : lanes + 128]
                            for i in range(8)
                        ]
                    )
                    place = field * LINES + group * 128
                    for j in range(8):
                        out_ref[
                            half * 8 + j, part * ZL : (part + 1) * ZL, place : place + 128
                        ] = chunks[j]


def spread(got, table_x):
    cells = jax.ShapeDtypeStruct((ROWS + LT, 128), F32)
    return pl.pallas_call(
        spread_kernel,
        out_shape=(
            jax.ShapeDtypeStruct((N_SLAB, 2 * ZL, 2 * LINES), BF),
            jax.ShapeDtypeStruct((LIST,), jnp.int32),
            jax.ShapeDtypeStruct((LT, 128), jnp.int32),
            cells,
            cells,
        ),
        in_specs=[VMEM] * 2,
        out_specs=(VMEM, SMEM, SMEM, VMEM, VMEM),
        scratch_shapes=[
            pltpu.VMEM((LT, 128), jnp.int32),
            pltpu.SemaphoreType.DMA(()),
            pltpu.VMEM((NX, 2 * HALF), BF),
        ]
        + [pltpu.VMEM((TILES * TALL, 128), F32)] * (2 * SETS),
        compiler_params=PARAMS,
        name="spread",
    )(got, table_x)


def spectral_kernel(cols_ref, table_ref, filter_ref, out_ref, grad_ref, mode_ref):
    table = table_ref[...]
    cols = cols_ref[...].reshape(2 * NZ, 2 * LINES)
    mode_ref[...] = lax.dot_general(cols, table, TN, preferred_element_type=F32).astype(BF)
    filtered, cot_spec = [], []
    for c in range(CL):
        filt = filter_ref[c * KX : (c + 1) * KX].astype(F32)
        fr, fi = filt[:, 0, :], filt[:, 1, :]
        grad_r = jnp.zeros((KX, NZ), F32)
        grad_i = jnp.zeros((KX, NZ), F32)
        for y in range(NY):
            first = (c * NY + y) * KX
            spec = mode_ref[first : first + KX, :].astype(F32)
            cot = mode_ref[LINES + first : LINES + first + KX, :].astype(F32)
            sr, si = spec[:, :NZ], spec[:, NZ:]
            gr, gi = cot[:, :NZ], cot[:, NZ:]
            filtered.append(jnp.concatenate([sr * fr - si * fi, sr * fi + si * fr], axis=1).astype(BF))
            cot_spec.append(jnp.concatenate([gr * fr + gi * fi, gi * fr - gr * fi], axis=1).astype(BF))
            grad_r = grad_r + (gr * sr + gi * si)
            grad_i = grad_i + (gi * sr - gr * si)
        grad_ref[c * KX : (c + 1) * KX, 0, :] = grad_r
        grad_ref[c * KX : (c + 1) * KX, 1, :] = grad_i
    for field, parts in enumerate((filtered, cot_spec)):
        planes = lax.dot_general(
            table, jnp.concatenate(parts, axis=0), NT, preferred_element_type=F32
        )
        out_ref[:, :, field * LINES : (field + 1) * LINES] = planes.astype(BF).reshape(
            N_SLAB, 2 * ZL, LINES
        )


def spectral(cols, table_z, filters):
    return pl.pallas_call(
        spectral_kernel,
        out_shape=(
            jax.ShapeDtypeStruct((N_SLAB, 2 * ZL, 2 * LINES), BF),
            jax.ShapeDtypeStruct((CL * KX, 2, NZ), F32),
        ),
        in_specs=[VMEM] * 3,
        out_specs=(VMEM,) * 2,
        scratch_shapes=[pltpu.VMEM((2 * LINES, 2 * NZ), BF)],
        compiler_params=PARAMS,
        name="spectral",
    )(cols, table_z, filters)


def gather_kernel(
    list_ref, info_ref, plane_ref, table_ref, cell_ref, half_ref, out_ref, mode_ref, field_ref, *wide_refs
):
    for field in range(2):
        for part in range(2):
            for group in range(CL * NY // 8):
                place = field * LINES + group * 128
                for half in range(2):
                    chunks = swap_chunks(
                        [
                            plane_ref[
                                half * 8 + j, part * ZL : (part + 1) * ZL, place : place + 128
                            ]
                            for j in range(8)
                        ]
                    )
                    lanes = part * NX + half * 128
                    for i in range(8):
                        first = field * HALF + (group * 8 + i) * ZL
                        mode_ref[first : first + ZL, lanes : lanes + 128] = chunks[i]
    for field in range(2):
        cells = lax.dot_general(
            table_ref[...],
            mode_ref[field * HALF : (field + 1) * HALF, :],
            NT,
            preferred_element_type=F32,
        )
        if field == 0:
            cells = cells * INV
        for pair in range(CL // 2):
            lanes = slice(pair * 128, (pair + 1) * 128)
            for col in range(2):
                first = 2 * col * 2 * TILES
                swapped = swap_halves(
                    cells[first : first + 2 * TILES, lanes],
                    cells[first + 2 * TILES : first + 4 * TILES, lanes],
                )
                for n in range(2):
                    wide_refs[col][
                        pl.ds(field * CL + 2 * pair + n, 2 * TILES, stride=FC), :
                    ] = swapped[n]
    for col in range(2):
        field_ref[:, col * 128 : (col + 1) * 128] = wide_refs[col][...].astype(BF)
    out_ref[...] = jnp.zeros_like(out_ref)
    block = 2.0 * (lax.broadcasted_iota(jnp.int32, (FC, 128), 1) // BLK).astype(F32)

    def some_rows(step, carry):
        lines = line_numbers(NX, BF)
        for pair in range(0, GROUP, 2):
            rows, places, picks = [], [], []
            for n in range(2):
                row = list_ref[step * GROUP + pair + n]
                row = jnp.where(row == ROWS, 0, row)
                rows.append(row)
                places += tile_rows(info_ref, row)
                picks.append(one_hot(cell_ref[pl.ds(row, 1), :], lines))
            found = jnp.dot(
                jnp.concatenate([field_ref[pl.ds(place, TALL), :] for place in places], axis=0),
                jnp.concatenate(picks, axis=1),
                preferred_element_type=F32,
            )
            for n, row in enumerate(rows):
                wanted = block + jnp.broadcast_to(half_ref[pl.ds(row, 1), :], (FC, 128))
                kept = jnp.zeros((FC, 128), F32)
                for k in range(2 * PER_ROW):
                    first = n * PER_ROW * TALL + k * FC
                    kept = jnp.where(
                        wanted == float(k),
                        found[first : first + FC, n * 128 : (n + 1) * 128],
                        kept,
                    )
                out_ref[row >> 3, row & (LT - 1)] = kept.astype(BF)
        return carry

    lax.fori_loop(0, list_ref[LIST - 1], some_rows, 0)


def gather(rows, infos, planes, table_x, cells, halves):
    return pl.pallas_call(
        gather_kernel,
        out_shape=jax.ShapeDtypeStruct((N_ROW, LT, FC, 128), BF),
        in_specs=[SMEM] * 2 + [VMEM] * 4,
        out_specs=VMEM,
        scratch_shapes=[
            pltpu.VMEM((2 * HALF, 2 * NX), BF),
            pltpu.VMEM((TILES * TALL, NX), BF),
            pltpu.VMEM((TILES * TALL, 128), F32),
            pltpu.VMEM((TILES * TALL, 128), F32),
        ],
        compiler_params=PARAMS,
        name="gather",
    )(rows, infos, planes, table_x, cells, halves)


def on_device(atom_feats, cotangent, filter_modes, block_tiles, cell_offsets, live_counts):
    table_x, table_z = make_tables()

    def over(axis, values):
        return lax.all_to_all(values, axis, split_axis=0, concat_axis=0, tiled=True)

    got = over("row", pack(atom_feats, cotangent, block_tiles, cell_offsets, live_counts))
    cols, rows, infos, cells, halves = spread(got, table_x)
    planes, grad = spectral(over("slab", cols), table_z, filter_modes.reshape(CL * KX, 2, NZ))
    found = gather(rows, infos, over("slab", planes), table_x, cells, halves)
    long_range, grad_feats = unpack(over("row", found))
    return (long_range, grad_feats, grad.reshape(CL, KX, 2, NZ))


def solution(mesh):
    in_specs = (
        P(None, ("slab", "row")),
        P(None, ("slab", "row")),
        P("row", "slab", None, None),
        P(("slab", "row"), None),
        P(("slab", "row")),
        P(("slab", "row")),
    )
    out_specs = (P(None, ("slab", "row")), P(None, ("slab", "row")), P("row", "slab", None, None))
    return jax.shard_map(
        on_device, mesh=mesh, in_specs=in_specs, out_specs=out_specs, check_vma=False
    )
```

```python
import jax
import jax.numpy as jnp
import numpy as np
from jax import lax
from jax.experimental import pallas as pl
from jax.experimental.pallas import tpu as pltpu
from jax.sharding import PartitionSpec as P

C = 128
NX = 256
NZ = 256
NY = 4
BLK = 32
N_SLAB = 16
N_ROW = 32
CL = C // N_ROW
FC = 2 * CL
KX = NX // N_SLAB
ZL = NZ // N_SLAB
A_DEV = 1024
LT = A_DEV // 128
BLOCKS = A_DEV // BLK
ZY = NY * ZL
HALF = CL * ZY
LINES = CL * NY * KX
INV = 1.0 / (NX * NZ)
PACK = 16
ROWS = N_ROW * LT
GROUP = 32
TILES = N_ROW
QUARTER = 4
PER_ROW = 128 // BLK
TALL = 2 * FC
SETS = 2
PIECES = 8
LIST = ROWS + GROUP + LT
BF = jnp.bfloat16
F32 = jnp.float32
NT = (((1,), (1,)), ((), ()))
TN = (((0,), (0,)), ((), ()))
VMEM = pl.BlockSpec(memory_space=pltpu.VMEM)
SMEM = pl.BlockSpec(memory_space=pltpu.SMEM)
HBM = pl.BlockSpec(memory_space=pltpu.HBM)
PARAMS = pltpu.CompilerParams(vmem_limit_bytes=32 << 20)


def trig_table(length):
    n = np.arange(length)
    angles = (np.outer(n, n) % length) * (2.0 * np.pi / length)
    return np.cos(angles), np.sin(angles)


def make_tables():
    cos_x, sin_x = trig_table(NX)
    cos_z, sin_z = trig_table(NZ)
    table_x = np.concatenate([cos_x, -sin_x], axis=1)
    upper = np.concatenate([cos_z, -sin_z], axis=1)
    lower = np.concatenate([sin_z, cos_z], axis=1)
    table_z = np.concatenate([upper, lower], axis=0)
    table_x = table_x.reshape(TILES, 2, QUARTER, 2 * NX).transpose(2, 0, 1, 3).reshape(NX, 2 * NX)
    table_z = table_z.reshape(2, N_SLAB, ZL, 2 * NZ).transpose(1, 0, 2, 3).reshape(2 * NZ, 2 * NZ)
    return jnp.asarray(table_x.astype(np.float32)).astype(BF), jnp.asarray(
        table_z.astype(np.float32)
    ).astype(BF)


def swap_chunks(parts):
    parts = list(parts)
    chunk = lax.broadcasted_iota(jnp.int32, parts[0].shape, 1) // KX
    for step in (1, 2, 4):
        upper = (chunk & step) != 0
        for i in range(8):
            if i & step:
                continue
            first, second = parts[i], parts[i | step]
            parts[i] = jnp.where(upper, pltpu.roll(second, step * KX, 1), first)
            parts[i | step] = jnp.where(upper, second, pltpu.roll(first, 128 - step * KX, 1))
    return parts


def encode_cells(cells, live):
    value = 1.0 + (cells & 127).astype(F32) * (1.0 / 128.0)
    for bit in range(6):
        value = value * jnp.where((cells >> (7 + bit)) & 1 == 1, F32(2.0 ** (1 << bit)), F32(1.0))
    value = value * jnp.where((cells >> 13) & 1 == 1, F32(1.0), F32(2.0**-64))
    return jnp.where(live, value, 0.0).astype(BF)


def decode_cells(code):
    value = code.astype(F32)
    live = value > 0.0
    top = value >= 1.0
    value = jnp.where(top, value, value * 2.0**64)
    high = jnp.where(top, 64, 0)
    for bit in range(5, -1, -1):
        over = value >= 2.0 ** (1 << bit)
        value = jnp.where(over, value * 2.0 ** -(1 << bit), value)
        high = high + jnp.where(over, 1 << bit, 0)
    low = ((value - 1.0) * 128.0).astype(jnp.int32)
    return jnp.where(live, high * 128 + low, -1)


def pack_kernel(
    tile_hbm, live_hbm, feat_hbm, cot_hbm, offset_hbm, out_hbm,
    tile_ref, live_ref, feat_ref, cot_ref, offset_ref, out_ref, sems,
):
    size = C // PIECES
    small = [
        pltpu.make_async_copy(source, held, sems.at[3 * PIECES + n])
        for n, (source, held) in enumerate(
            ((tile_hbm, tile_ref), (live_hbm, live_ref), (offset_hbm, offset_ref))
        )
    ]
    copies = []
    for piece in range(PIECES):
        rows = pl.ds(piece * size, size)
        for n, (source, held) in enumerate(((feat_hbm, feat_ref), (cot_hbm, cot_ref))):
            copies.append(
                pltpu.make_async_copy(source.at[rows], held.at[rows], sems.at[2 * piece + n])
            )
    for copy in small + copies:
        copy.start()
    for copy in small:
        copy.wait()
    shape = (LT, 128)
    slot = lax.broadcasted_iota(jnp.int32, shape, 0) * 128 + lax.broadcasted_iota(
        jnp.int32, shape, 1
    )
    block = slot // BLK
    tile = jnp.zeros(shape, jnp.int32)
    for n in range(BLOCKS):
        tile = jnp.where(block == n, tile_ref[n], tile)
    offset = offset_ref[...]
    zy_cell = ((offset >> 3) & (NY - 1)) * ZL + (offset >> 5)
    cells = zy_cell * NX + tile * (NX // N_ROW) + (offset & 7)
    code = encode_cells(cells, slot < live_ref[0, 0])
    for owner in range(N_ROW):
        out_ref[owner, LT] = code
    low = lax.broadcasted_iota(jnp.int32, (FC, 128), 0) < CL
    sent = []
    for piece in range(PIECES):
        copies[2 * piece].wait()
        copies[2 * piece + 1].wait()
        for pair in range(piece * size // FC, (piece + 1) * size // FC):
            rows = slice(pair * FC, (pair + 1) * FC)
            for j in range(LT):
                lanes = slice(j * 128, (j + 1) * 128)
                feat = feat_ref[rows, lanes].astype(F32)
                cot = cot_ref[rows, lanes].astype(F32)
                out_ref[2 * pair, j] = jnp.where(low, feat, pltpu.roll(cot, CL, 0)).astype(BF)
                out_ref[2 * pair + 1, j] = jnp.where(low, pltpu.roll(feat, CL, 0), cot).astype(BF)
        owners = pl.ds(piece * N_ROW // PIECES, N_ROW // PIECES)
        sent.append(
            pltpu.make_async_copy(
                out_ref.at[owners], out_hbm.at[owners], sems.at[2 * PIECES + piece]
            )
        )
        sent[-1].start()
    for copy in sent:
        copy.wait()


def pack(atom_feats, cotangent, block_tiles, cell_offsets, live_counts):
    return pl.pallas_call(
        pack_kernel,
        out_shape=jax.ShapeDtypeStruct((N_ROW, LT + 1, FC, 128), BF),
        in_specs=[HBM] * 5,
        out_specs=HBM,
        scratch_shapes=[
            pltpu.SMEM((BLOCKS,), jnp.int32),
            pltpu.SMEM((1, 1), jnp.int32),
            pltpu.VMEM((C, A_DEV), BF),
            pltpu.VMEM((C, A_DEV), BF),
            pltpu.VMEM((LT, 128), jnp.int32),
            pltpu.VMEM((N_ROW, LT + 1, FC, 128), BF),
            pltpu.SemaphoreType.DMA((3 * PIECES + 3,)),
        ],
        compiler_params=pltpu.CompilerParams(vmem_limit_bytes=60 * 1024 * 1024),
        name="pack",
    )(
        block_tiles.reshape(BLOCKS),
        live_counts.reshape(1, 1),
        atom_feats,
        cotangent,
        cell_offsets.reshape(LT, 128),
    )


def unpack_kernel(in_ref, feat_hbm, cot_hbm, feat_ref, cot_ref, sems):
    low = lax.broadcasted_iota(jnp.int32, (FC, 128), 0) < CL
    size = C // PIECES
    sent = []
    for piece in range(PIECES):
        for pair in range(piece * size // FC, (piece + 1) * size // FC):
            rows = slice(pair * FC, (pair + 1) * FC)
            for j in range(LT):
                lanes = slice(j * 128, (j + 1) * 128)
                first = in_ref[2 * pair, j].astype(F32)
                second = in_ref[2 * pair + 1, j].astype(F32)
                feat_ref[rows, lanes] = jnp.where(low, first, pltpu.roll(second, CL, 0)).astype(BF)
                cot_ref[rows, lanes] = jnp.where(low, pltpu.roll(first, CL, 0), second).astype(BF)
        rows = pl.ds(piece * size, size)
        for n, (held, target) in enumerate(((feat_ref, feat_hbm), (cot_ref, cot_hbm))):
            sent.append(
                pltpu.make_async_copy(held.at[rows], target.at[rows], sems.at[2 * piece + n])
            )
            sent[-1].start()
    for copy in sent:
        copy.wait()


def unpack(values):
    shape = jax.ShapeDtypeStruct((C, A_DEV), BF)
    return pl.pallas_call(
        unpack_kernel,
        out_shape=(shape, shape),
        in_specs=[VMEM],
        out_specs=(HBM, HBM),
        scratch_shapes=[
            pltpu.VMEM((C, A_DEV), BF),
            pltpu.VMEM((C, A_DEV), BF),
            pltpu.SemaphoreType.DMA((2 * PIECES,)),
        ],
        compiler_params=PARAMS,
        name="unpack",
    )(values)


def line_numbers(count, dtype):
    return [
        (lax.broadcasted_iota(jnp.int32, (PACK, 128), 0) + first).astype(F32).astype(dtype)
        for first in range(0, count, PACK)
    ]


def one_hot(row, lines):
    cell = jnp.broadcast_to(row, (PACK, 128)).astype(BF)
    one, zero = jnp.ones((PACK, 128), BF), jnp.zeros((PACK, 128), BF)
    return jnp.concatenate([jnp.where(cell == line, one, zero) for line in lines], axis=0)


def swap_halves(first, second):
    low = lax.broadcasted_iota(jnp.int32, first.shape, 1) < 64
    return (
        jnp.where(low, first, pltpu.roll(second, 64, 1)),
        jnp.where(low, pltpu.roll(first, 64, 1), second),
    )


def tile_rows(info_ref, row):
    info = info_ref[row & (LT - 1), row >> 3]
    return [
        pl.multiple_of((info >> (5 * k)) & ((TILES - 1) * TALL), TALL) for k in range(PER_ROW)
    ]


def spread_kernel(
    got_ref, table_ref, out_ref, list_ref, info_ref, cell_ref, half_ref, held_ref, sem, mesh_ref, *accs
):
    lane = lax.broadcasted_iota(jnp.int32, (LT, 128), 1)
    cell_ref[ROWS : ROWS + LT, :] = jnp.full((LT, 128), -1.0, F32)
    half_ref[ROWS : ROWS + LT, :] = jnp.zeros((LT, 128), F32)
    infos = jnp.zeros((LT, 128), F32)
    total = jnp.int32(0)
    for src in range(N_ROW):
        cells = decode_cells(got_ref[src, LT])
        live = cells >= 0
        rows = slice(src * LT, (src + 1) * LT)
        x_cell = cells & (NX - 1)
        cell_ref[rows, :] = jnp.where(
            live, (x_cell & (QUARTER - 1)) * ZY + (cells >> 8), -1
        ).astype(F32)
        half_ref[rows, :] = ((x_cell >> 2) & 1).astype(F32)
        tile = ((x_cell >> 3) * TALL) << (5 * (lane // BLK))
        tiles = jnp.sum(
            jnp.where(live & (lane % BLK == 0), tile, 0).astype(F32), axis=1, keepdims=True
        )
        for j in range(LT):
            list_ref[total + j] = src * LT + j
        total = total + jnp.sum(jnp.where(live & (lane == 0), 1.0, 0.0)).astype(jnp.int32)
        infos = jnp.where(lane == src, jnp.broadcast_to(tiles, (LT, 128)), infos)
    held_ref[...] = infos.astype(jnp.int32)
    copy = pltpu.make_async_copy(held_ref, info_ref, sem)
    copy.start()
    for acc in accs:
        acc[...] = jnp.zeros_like(acc)
    copy.wait()
    for n in range(GROUP):
        list_ref[total + n] = ROWS
    steps = (total + GROUP - 1) // GROUP
    list_ref[LIST - 1] = steps

    zero = jnp.zeros((TALL, 128), BF)
    upper = (lax.broadcasted_iota(jnp.int32, (TALL, 128), 0) // FC).astype(F32).astype(BF)
    block = (lax.broadcasted_iota(jnp.int32, (TALL, 128), 1) // BLK).astype(F32).astype(BF)

    def some_rows(step, carry):
        lines = line_numbers(NX, BF)
        for pair in range(0, GROUP, 2):
            right, left, places = [], [], []
            for n in range(2):
                row = list_ref[step * GROUP + pair + n]
                held = jnp.minimum(row, ROWS - 1)
                values = got_ref[held >> 3, held & (LT - 1)].astype(F32)
                half = jnp.broadcast_to(half_ref[pl.ds(row, 1), :], (TALL, 128)).astype(BF)
                values = jnp.where(
                    half == upper, jnp.concatenate([values, values], axis=0).astype(BF), zero
                )
                right.append(one_hot(cell_ref[pl.ds(row, 1), :], lines))
                mine = [jnp.where(block == float(k), values, zero) for k in range(PER_ROW)]
                none = [zero] * PER_ROW
                left.append(jnp.concatenate(mine + none if n == 0 else none + mine, axis=0))
                places += tile_rows(info_ref, row)
            sums = lax.dot_general(
                jnp.concatenate(left, axis=1),
                jnp.concatenate(right, axis=1),
                NT,
                preferred_element_type=F32,
            )
            for k, place in enumerate(places):
                for col in range(2):
                    acc = accs[2 * (k % SETS) + col]
                    acc[pl.ds(place, TALL), :] += sums[
                        k * TALL : (k + 1) * TALL, col * 128 : (col + 1) * 128
                    ]
        return carry

    lax.fori_loop(0, steps, some_rows, 0)
    for col in range(2):
        accs[col][...] += accs[2 + col][...]
    for pair in range(FC // 2):
        for col in range(2):
            even, odd = (
                accs[col][pl.ds(2 * pair + n, 2 * TILES, stride=FC), :].astype(BF)
                for n in range(2)
            )
            for n, block_rows in enumerate(swap_halves(even, odd)):
                first = (2 * col + n) * 2 * TILES
                mesh_ref[first : first + 2 * TILES, pair * 128 : (pair + 1) * 128] = block_rows
    for field in range(2):
        rows = lax.dot_general(
            mesh_ref[:, field * HALF : (field + 1) * HALF],
            table_ref[...],
            TN,
            preferred_element_type=F32,
        )
        rows = (rows * INV if field == 1 else rows).astype(BF)
        for part in range(2):
            for group in range(CL * NY // 8):
                for half in range(2):
                    lanes = part * NX + half * 128
                    chunks = swap_chunks(
                        [
                            rows[(group * 8 + i) * ZL : (group * 8 + i + 1) * ZL, lanes : lanes + 128]
                            for i in range(8)
                        ]
                    )
                    place = field * LINES + group * 128
                    for j in range(8):
                        out_ref[
                            half * 8 + j, part * ZL : (part + 1) * ZL, place : place + 128
                        ] = chunks[j]


def spread(got, table_x):
    cells = jax.ShapeDtypeStruct((ROWS + LT, 128), F32)
    return pl.pallas_call(
        spread_kernel,
        out_shape=(
            jax.ShapeDtypeStruct((N_SLAB, 2 * ZL, 2 * LINES), BF),
            jax.ShapeDtypeStruct((LIST,), jnp.int32),
            jax.ShapeDtypeStruct((LT, 128), jnp.int32),
            cells,
            cells,
        ),
        in_specs=[VMEM] * 2,
        out_specs=(VMEM, SMEM, SMEM, VMEM, VMEM),
        scratch_shapes=[
            pltpu.VMEM((LT, 128), jnp.int32),
            pltpu.SemaphoreType.DMA(()),
            pltpu.VMEM((NX, 2 * HALF), BF),
        ]
        + [pltpu.VMEM((TILES * TALL, 128), F32)] * (2 * SETS),
        compiler_params=PARAMS,
        name="spread",
    )(got, table_x)


def spectral_kernel(cols_ref, table_ref, filter_ref, out_ref, grad_ref, mode_ref):
    table = table_ref[...]
    cols = cols_ref[...].reshape(2 * NZ, 2 * LINES)
    mode_ref[...] = lax.dot_general(cols, table, TN, preferred_element_type=F32).astype(BF)
    filtered, cot_spec = [], []
    for c in range(CL):
        filt = filter_ref[c * KX : (c + 1) * KX, :].astype(F32)
        fr, fi = filt[:, :NZ], filt[:, NZ:]
        grad_r = jnp.zeros((KX, NZ), F32)
        grad_i = jnp.zeros((KX, NZ), F32)
        for y in range(NY):
            first = (c * NY + y) * KX
            spec = mode_ref[first : first + KX, :].astype(F32)
            cot = mode_ref[LINES + first : LINES + first + KX, :].astype(F32)
            sr, si = spec[:, :NZ], spec[:, NZ:]
            gr, gi = cot[:, :NZ], cot[:, NZ:]
            filtered.append(jnp.concatenate([sr * fr - si * fi, sr * fi + si * fr], axis=1).astype(BF))
            cot_spec.append(jnp.concatenate([gr * fr + gi * fi, gi * fr - gr * fi], axis=1).astype(BF))
            grad_r = grad_r + (gr * sr + gi * si)
            grad_i = grad_i + (gi * sr - gr * si)
        grad_ref[c * KX : (c + 1) * KX, :NZ] = grad_r
        grad_ref[c * KX : (c + 1) * KX, NZ:] = grad_i
    for field, parts in enumerate((filtered, cot_spec)):
        planes = lax.dot_general(
            table, jnp.concatenate(parts, axis=0), NT, preferred_element_type=F32
        )
        out_ref[:, :, field * LINES : (field + 1) * LINES] = planes.astype(BF).reshape(
            N_SLAB, 2 * ZL, LINES
        )


def spectral(cols, table_z, filters):
    return pl.pallas_call(
        spectral_kernel,
        out_shape=(
            jax.ShapeDtypeStruct((N_SLAB, 2 * ZL, 2 * LINES), BF),
            jax.ShapeDtypeStruct((CL * KX, 2 * NZ), F32),
        ),
        in_specs=[VMEM] * 3,
        out_specs=(VMEM,) * 2,
        scratch_shapes=[pltpu.VMEM((2 * LINES, 2 * NZ), BF)],
        compiler_params=PARAMS,
        name="spectral",
    )(cols, table_z, filters)


def gather_kernel(
    list_ref, info_ref, plane_ref, table_ref, cell_ref, half_ref, out_ref, mode_ref, field_ref, *wide_refs
):
    for field in range(2):
        for part in range(2):
            for group in range(CL * NY // 8):
                place = field * LINES + group * 128
                for half in range(2):
                    chunks = swap_chunks(
                        [
                            plane_ref[
                                half * 8 + j, part * ZL : (part + 1) * ZL, place : place + 128
                            ]
                            for j in range(8)
                        ]
                    )
                    lanes = part * NX + half * 128
                    for i in range(8):
                        first = field * HALF + (group * 8 + i) * ZL
                        mode_ref[first : first + ZL, lanes : lanes + 128] = chunks[i]
    for field in range(2):
        cells = lax.dot_general(
            table_ref[...],
            mode_ref[field * HALF : (field + 1) * HALF, :],
            NT,
            preferred_element_type=F32,
        )
        if field == 0:
            cells = cells * INV
        for pair in range(CL // 2):
            lanes = slice(pair * 128, (pair + 1) * 128)
            for col in range(2):
                first = 2 * col * 2 * TILES
                swapped = swap_halves(
                    cells[first : first + 2 * TILES, lanes],
                    cells[first + 2 * TILES : first + 4 * TILES, lanes],
                )
                for n in range(2):
                    wide_refs[col][
                        pl.ds(field * CL + 2 * pair + n, 2 * TILES, stride=FC), :
                    ] = swapped[n]
    for col in range(2):
        field_ref[:, col * 128 : (col + 1) * 128] = wide_refs[col][...].astype(BF)
    out_ref[...] = jnp.zeros_like(out_ref)
    block = 2.0 * (lax.broadcasted_iota(jnp.int32, (FC, 128), 1) // BLK).astype(F32)

    def some_rows(step, carry):
        lines = line_numbers(NX, BF)
        for pair in range(0, GROUP, 2):
            rows, places, picks = [], [], []
            for n in range(2):
                row = list_ref[step * GROUP + pair + n]
                row = jnp.where(row == ROWS, 0, row)
                rows.append(row)
                places += tile_rows(info_ref, row)
                picks.append(one_hot(cell_ref[pl.ds(row, 1), :], lines))
            found = jnp.dot(
                jnp.concatenate([field_ref[pl.ds(place, TALL), :] for place in places], axis=0),
                jnp.concatenate(picks, axis=1),
                preferred_element_type=F32,
            )
            for n, row in enumerate(rows):
                wanted = block + jnp.broadcast_to(half_ref[pl.ds(row, 1), :], (FC, 128))
                kept = jnp.zeros((FC, 128), F32)
                for k in range(2 * PER_ROW):
                    first = n * PER_ROW * TALL + k * FC
                    kept = jnp.where(
                        wanted == float(k),
                        found[first : first + FC, n * 128 : (n + 1) * 128],
                        kept,
                    )
                out_ref[row >> 3, row & (LT - 1)] = kept.astype(BF)
        return carry

    lax.fori_loop(0, list_ref[LIST - 1], some_rows, 0)


def gather(rows, infos, planes, table_x, cells, halves):
    return pl.pallas_call(
        gather_kernel,
        out_shape=jax.ShapeDtypeStruct((N_ROW, LT, FC, 128), BF),
        in_specs=[SMEM] * 2 + [VMEM] * 4,
        out_specs=VMEM,
        scratch_shapes=[
            pltpu.VMEM((2 * HALF, 2 * NX), BF),
            pltpu.VMEM((TILES * TALL, NX), BF),
            pltpu.VMEM((TILES * TALL, 128), F32),
            pltpu.VMEM((TILES * TALL, 128), F32),
        ],
        compiler_params=PARAMS,
        name="gather",
    )(rows, infos, planes, table_x, cells, halves)


def on_device(atom_feats, cotangent, filter_modes, block_tiles, cell_offsets, live_counts):
    table_x, table_z = make_tables()

    def over(axis, values):
        return lax.all_to_all(values, axis, split_axis=0, concat_axis=0, tiled=True)

    got = over("row", pack(atom_feats, cotangent, block_tiles, cell_offsets, live_counts))
    cols, rows, infos, cells, halves = spread(got, table_x)
    planes, grad = spectral(over("slab", cols), table_z, filter_modes.reshape(CL * KX, 2 * NZ))
    found = gather(rows, infos, over("slab", planes), table_x, cells, halves)
    long_range, grad_feats = unpack(over("row", found))
    return (long_range, grad_feats, grad.reshape(CL, KX, 2, NZ))


def solution(mesh):
    in_specs = (
        P(None, ("slab", "row")),
        P(None, ("slab", "row")),
        P("row", "slab", None, None),
        P(("slab", "row"), None),
        P(("slab", "row")),
        P(("slab", "row")),
    )
    out_specs = (P(None, ("slab", "row")), P(None, ("slab", "row")), P("row", "slab", None, None))
    return jax.shard_map(
        on_device, mesh=mesh, in_specs=in_specs, out_specs=out_specs, check_vma=False
    )
```
